32 devices in a mesh: fsdp: 32 (over z, y, x, core).
Axes of the slice: x: 2, y: 2, z: 4, core: 2. Of those that a mesh axis runs over, the one named last changes fastest.
Arguments:
- inputs: bfloat16 [64, 1024, 1280], P('fsdp'), may hold values from -6 to 6
- block_ids: int32 [64, 1024], P('fsdp'), may hold values from 0 to 3, never falling along the last dimension, each value on 1 to 512 neighbouring positions
- cotangent: bfloat16 [64, 1024, 1280], P('fsdp'), may hold values from -9 to 9
- first_gain: bfloat16 [1280], P('fsdp'), may hold values from 0.25 to 1.75
- query_weight: bfloat16 [1280, 1280], P(None, 'fsdp'), may hold values from -0.15625 to 0.15625
- key_weight: bfloat16 [1280, 1280], P(None, 'fsdp'), may hold values from -0.15625 to 0.15625
- value_weight: bfloat16 [1280, 1280], P(None, 'fsdp'), may hold values from -0.15625 to 0.15625
- output_weight: bfloat16 [1280, 1280], P(None, 'fsdp'), may hold values from -1.25 to 1.25
- second_gain: bfloat16 [1280], P('fsdp'), may hold values from 0.25 to 1.75
- up_weight: bfloat16 [1280, 1280], P(None, 'fsdp'), may hold values from -0.15625 to 0.15625
- down_weight: bfloat16 [1280, 1280], P(None, 'fsdp'), may hold values from -0.15625 to 0.15625
- query_scale: float32 [80], replicated, may hold values from 1 to 3
Outputs:
- layer_output: bfloat16 [64, 1024, 1280], P('fsdp')
- grad_inputs: float32 [64, 1024, 1280], P('fsdp')
- grad_first_gain: float32 [1280], P('fsdp')
- grad_query_weight: float32 [1280, 1280], P(None, 'fsdp')
- grad_key_weight: float32 [1280, 1280], P(None, 'fsdp')
- grad_value_weight: float32 [1280, 1280], P(None, 'fsdp')
- grad_output_weight: float32 [1280, 1280], P(None, 'fsdp')
- grad_second_gain: float32 [1280], P('fsdp')
- grad_up_weight: float32 [1280, 1280], P(None, 'fsdp')
- grad_down_weight: float32 [1280, 1280], P(None, 'fsdp')
- grad_query_scale: float32 [80], replicated
The draws below stay inside these ranges and needn't reach their ends.
Inputs may be any that keep to these rules, and one draw needn't show every extreme that they name: `block_ids`: within a sequence the ids never fall, each of the 4 ids is used, by 1 to 512 consecutive tokens.
All inputs are finite; a program needn't handle non-finite values.
Results may differ from the reference program's by a relative error of at most 0.013.
The reference program's roundings to bfloat16 on the way count: a program that leaves them out, or rounds other values in their place, can miss the bound.
Values may be sent and summed in bfloat16 or wider, within the bound.
No kernel may reach another device: no remote copies, remote signals or barrier semaphores. Data moves between devices by JAX's collectives and lax.ppermute only.
A program may use at most 576 MiB of HBM per device.

```python
import math
import jax
import jax.numpy as jnp
import numpy as np
from jax import lax

D = 1280
HEADS = 16
HEAD_DIM = 80
FF = 1280
SEQ_LEN = 1024
BLOCK = 256
NBLK = 4
SEQS = 64


def draw_cotangent(key, part):
    sample = jnp.clip(jax.random.normal(key, (SEQS, SEQ_LEN, D), jnp.float32), -6.0, 6.0)
    position = jnp.arange(SEQS).astype(jnp.float32) / max(SEQS - 1, 1)
    growth = 0.5 + position
    return (sample * growth[:, None, None]).astype(jnp.bfloat16)


def steps_of(rng, extent, pieces, least, high):
    level = 1.0
    for axis_at, blocks in pieces:
        draws = jax.random.uniform(jax.random.fold_in(jax.random.fold_in(rng, 6), axis_at), (blocks,), jnp.float32, least / len(pieces), high / len(pieces))
        level = level * jnp.repeat(jnp.exp(draws), extent[axis_at] // blocks).reshape((-1,) + (1,) * (len(extent) - 1 - axis_at))
    return level


def split_up(count, total, most, skew):
    portions = [(1 << 20) // math.isqrt(standing ** skew) + 1 for standing in range(2, count + 1)]
    rest, counts = total - most - (count - 1), [1] * (count - 1)
    while rest > 0:
        free = [i for i in range(count - 1) if counts[i] < most]
        mass, left = sum([portions[i] for i in free]), rest
        for i in free:
            more = min(most - counts[i], max(1, left * portions[i] // mass), rest)
            counts[i] = counts[i] + more
            rest = rest - more
    return np.array([most] + counts)


def ragged(rng, number_of, total, reach, slope):
    if number_of == 2:
        one = jax.random.randint(rng, (), max(1, total - reach), min(reach, total - 1) + 1)
        return jnp.stack([one, total - one])
    tallies = jnp.asarray(split_up(number_of, total, reach, slope), jnp.int32)
    twos = (number_of - 1) // 2
    source_of, taker = tallies[1:1 + 2 * twos:2], tallies[2:2 + 2 * twos:2]
    margin = jnp.minimum(source_of - 1, reach - taker)
    shifted = jax.random.randint(jax.random.fold_in(rng, 1), (twos,), 0, 1 << 20) % (margin + 1)
    tallies = tallies.at[1:1 + 2 * twos:2].set(source_of - shifted).at[2:2 + 2 * twos:2].set(taker + shifted)
    return tallies[jax.random.permutation(jax.random.fold_in(rng, 2), number_of)]


def noise(own_key, dims, scale, reach, pieces=(), dtype=jnp.bfloat16):
    values = scale * jax.random.normal(own_key, dims, jnp.float32)
    if pieces:
        values = values * steps_of(own_key, dims, pieces, -0.22, 0.18)
    return jnp.clip(values, -reach, reach).astype(dtype)


def setup_inputs(seed: int = 0) -> dict:
    splits = jax.random.split(jax.random.key(seed), 13)
    return {
        "inputs": noise(splits[0], (SEQS, SEQ_LEN, D), 1.0, 6.0, ((0, 32),)),
        "block_ids": jax.vmap(lambda own: jnp.searchsorted(jnp.cumsum(ragged(own, NBLK, SEQ_LEN, 2 * BLOCK, 2)), jnp.arange(SEQ_LEN), side="right"))(jax.random.split(splits[1], SEQS)).reshape((SEQS, SEQ_LEN)).astype(jnp.int32),
        "cotangent": draw_cotangent(jax.random.fold_in(splits[12], 71), 0),
        "first_gain": jnp.clip(1.0 + 0.15 * jax.random.normal(splits[3], (D,), jnp.float32), 0.25, 1.75).astype(jnp.bfloat16),
        "query_weight": noise(splits[4], (D, D), D ** -0.5, 0.15625, ((1, 32),)),
        "key_weight": noise(splits[5], (D, D), D ** -0.5, 0.15625, ((1, 32),)),
        "value_weight": noise(splits[6], (D, D), D ** -0.5, 0.15625, ((1, 32),)),
        "output_weight": noise(splits[7], (D, D), (D // 64) ** -0.5, 1.25, ((1, 32),)),
        "second_gain": jnp.clip(1.0 + 0.15 * jax.random.normal(splits[8], (D,), jnp.float32), 0.25, 1.75).astype(jnp.bfloat16),
        "up_weight": noise(splits[9], (D, FF), D ** -0.5, 0.15625, ((1, 32),)),
        "down_weight": noise(splits[10], (FF, D), FF ** -0.5, 0.15625, ((1, 32),)),
        "query_scale": jnp.clip(jnp.exp(jax.random.uniform(splits[11], (HEAD_DIM,), jnp.float32, math.log(1.0), math.log(3.0))), 1.0, 3.0),
    }


@jax.custom_vjp
def low(v):
    return lax.optimization_barrier(v.astype(jnp.bfloat16)).astype(jnp.float32)

@jax.custom_vjp
def low_back(v):
    return v

def low_keep(v):
    return (low(v), None)

def low_pass(kept, grad):
    return (grad,)

def back_keep(v):
    return (v, None)

def back_low(kept, grad):
    return (low(grad),)
low.defvjp(low_keep, low_pass)
low_back.defvjp(back_keep, back_low)

def highest_dot(left, right):
    return jnp.dot(left, right, preferred_element_type=jnp.float32, precision=lax.Precision.HIGHEST)

def rms_norm(source, gain):
    root = lax.rsqrt(lax.optimization_barrier(jnp.mean(source * source, axis=-1, keepdims=True)) + 1e-06)
    return source * root * gain

def sequence_layer(source, sequence_ids, params):
    first_gain, query_weight, key_weight, value_weight, output_weight, second_gain, up_weight, down_weight, query_scale = params
    length = source.shape[0]
    normed = low(rms_norm(source, first_gain))
    query_heads = low_back(highest_dot(normed, query_weight)).reshape(length, HEADS, HEAD_DIM)
    key_heads = low(low_back(highest_dot(normed, key_weight))).reshape(length, HEADS, HEAD_DIM)
    value_heads = low(low_back(highest_dot(normed, value_weight))).reshape(length, HEADS, HEAD_DIM)
    scaled = low(query_heads * (query_scale / math.sqrt(HEAD_DIM)))
    scores = low_back(jnp.einsum('qhd,khd->hqk', scaled, key_heads, precision=lax.Precision.HIGHEST))
    visible = sequence_ids[None, :] <= sequence_ids[:, None]
    scores = jnp.where(visible[None], scores, -1e+30)
    probability = low(jax.nn.softmax(scores, axis=-1))
    context = jnp.einsum('hqk,khd->qhd', probability, value_heads, precision=lax.Precision.HIGHEST)
    context = low(low_back(context)).reshape(length, D)
    hidden = source + low_back(highest_dot(context, output_weight))
    normed_second = low(rms_norm(hidden, second_gain))
    upward = low_back(highest_dot(normed_second, up_weight))
    activated = low(jax.nn.silu(upward))
    return hidden + low_back(highest_dot(activated, down_weight))

def reference(inputs, block_ids, cotangent, first_gain, query_weight, key_weight, value_weight, output_weight, second_gain, up_weight, down_weight, query_scale):
    params = tuple((member.astype(jnp.float32) for member in (first_gain, query_weight, key_weight, value_weight, output_weight, second_gain, up_weight, down_weight, query_scale)))

    def forward(sources, weights):

        def step(running, members):
            return (running, sequence_layer(members[0], members[1], weights))
        _, results = lax.scan(jax.checkpoint(step), jnp.zeros((), jnp.float32), (sources, block_ids))
        return results
    results, pullback = jax.vjp(forward, inputs.astype(jnp.float32), params)
    grad_source, gradients = pullback(cotangent.astype(jnp.float32))
    return (results.astype(jnp.bfloat16), grad_source, gradients[0], gradients[1], gradients[2], gradients[3], gradients[4], gradients[5], gradients[6], gradients[7], gradients[8])
```

```python
import functools
import math

import jax
import jax.numpy as jnp
from jax import lax
from jax.experimental import pallas as pl
from jax.experimental.pallas import tpu as pltpu
from jax.sharding import PartitionSpec as P

EPSILON = 1e-06
AXIS = "fsdp"
BLOCKS = 4
TILE = 256
EXTRA = 16
HEADS_PER_STEP = 4
LOW = jnp.bfloat16
LOG2E = math.log2(math.e)
LN2 = math.log(2.0)
NN = (((1,), (0,)), ((), ()))
NT = (((1,), (1,)), ((), ()))
TN = (((0,), (0,)), ((), ()))
TT = (((0,), (1,)), ((), ()))


def dot(left, right, dims):
    return lax.dot_general(left, right, dims, preferred_element_type=jnp.float32)


def three_rows(value, base, at):
    row = lax.broadcasted_iota(jnp.int32, (EXTRA, value.shape[1]), 0)
    first = value.astype(LOW).astype(jnp.float32)
    rest = value - first
    second = rest.astype(LOW).astype(jnp.float32)
    third = rest - second
    rows = jnp.where(row == at + 1, second, jnp.where(row == at + 2, third, base))
    return jnp.where(row == at, first, rows).astype(LOW)


def fold(x, op):
    return op(x.reshape(x.shape[0] // 8, 8, x.shape[1]), axis=0)


def for_each_tile(length, count_of, body):
    @pl.loop(0, length // TILE)
    def _(t):
        count = count_of(t)
        for n in range(1, length // TILE + 1):

            @pl.when(count == n)
            def _(n=n):
                body(pl.ds(pl.multiple_of(t * TILE, TILE), TILE), n)


def attention_forward_kernel(
    heads, depth, length, counts, q_ref, k_ref, v_ref, qx_ref, kx_ref, o_ref, lse_ref, kn, sb
):
    s = pl.program_id(1)
    for h in range(heads):
        kn[h] = jnp.concatenate([k_ref[h * depth : (h + 1) * depth, :], kx_ref[...]], axis=0).T

    def tile(qs, n):
        qx = qx_ref[:, qs]
        peaks = [None] * (heads + 1)
        for h in range(heads + 1):
            out = total = None
            if h > 0:
                peak = jnp.max(peaks[h - 1], axis=0, keepdims=True)
            for c in range(n):
                ks = slice(c * TILE, (c + 1) * TILE)
                if h < heads:
                    q = jnp.concatenate([q_ref[h * depth : (h + 1) * depth, qs], qx], axis=0)
                    scores = dot(kn[h, ks, :], q, NN)
                    sb[h % 2, ks, :] = scores
                    part = fold(scores, jnp.max)
                    peaks[h] = part if c == 0 else jnp.maximum(peaks[h], part)
                if h > 0:
                    p = jnp.exp2(sb[(h - 1) % 2, ks, :] - peak)
                    part = fold(p, jnp.sum)
                    total = part if c == 0 else total + part
                    part = dot(v_ref[(h - 1) * depth : h * depth, ks], p.astype(LOW), NN)
                    out = part if c == 0 else out + part
            if h > 0:
                total = jnp.sum(total, axis=0, keepdims=True)
                o_ref[(h - 1) * depth : h * depth, qs] = (out * (1.0 / total)).astype(LOW)
                lse_ref[h - 1, :, qs] = peak + jnp.log2(total)

    for_each_tile(length, lambda t: counts[s, t], tile)


def attention_forward(qkv, qx, kx, counts, depth, length):
    heads = HEADS_PER_STEP
    rows = qkv.shape[1]
    head_count, seqs = rows // depth, qkv.shape[2] // length
    group = heads * depth

    def third(i):
        return pl.BlockSpec((None, group, length), lambda h, s, counts: (i, h, s))

    extra = pl.BlockSpec((EXTRA, length), lambda h, s, counts: (0, s))
    return pl.pallas_call(
        functools.partial(attention_forward_kernel, heads, depth, length),
        grid_spec=pltpu.PrefetchScalarGridSpec(
            num_scalar_prefetch=1,
            grid=(head_count // heads, seqs),
            in_specs=[third(0), third(1), third(2), extra, extra],
            out_specs=[
                pl.BlockSpec((group, length), lambda h, s, counts: (h, s)),
                pl.BlockSpec((heads, 1, length), lambda h, s, counts: (h, 0, s)),
            ],
            scratch_shapes=[
                pltpu.VMEM((heads, length, depth + EXTRA), LOW),
                pltpu.VMEM((2, length, TILE), jnp.float32),
            ],
        ),
        out_shape=[
            jax.ShapeDtypeStruct((rows, seqs * length), LOW),
            jax.ShapeDtypeStruct((head_count, 1, seqs * length), jnp.float32),
        ],
        cost_estimate=pl.CostEstimate(
            flops=4 * head_count * 256 * length * length * seqs,
            bytes_accessed=8 * rows * seqs * length,
            transcendentals=head_count * length * length * seqs,
        ),
        name="attention_forward",
    )(counts, qkv, qkv, qkv, qx, kx)


def attention_backward_kernel(
    heads,
    depth,
    length,
    ahead,
    counts,
    q_ref,
    k_ref,
    v_ref,
    o_ref,
    do_ref,
    lse_ref,
    qx_ref,
    kx_ref,
    factor_ref,
    d_ref,
    scale_ref,
    kn,
    vn,
    dka,
    dva,
):
    s = pl.program_id(1)

    @pl.when((pl.program_id(0) == 0) & (s == 0))
    def _():
        scale_ref[...] = jnp.zeros_like(scale_ref)

    dka[...] = jnp.zeros_like(dka)
    dva[...] = jnp.zeros_like(dva)
    ones = jnp.where(lax.broadcasted_iota(jnp.int32, (EXTRA, length), 0) < 3, 1.0, 0.0).astype(LOW)
    for h in range(heads):
        hs = slice(h * depth, (h + 1) * depth)
        kn[h] = jnp.concatenate([k_ref[hs, :], kx_ref[...]], axis=0).T
        vn[h] = jnp.concatenate([v_ref[hs, :], ones], axis=0).T

    def tile(qs, n):
        base = qx_ref[:, qs].astype(jnp.float32)
        queries, grads = [], []
        items = [(h, c) for h in range(heads) for c in range(n)]

        def first(i):
            h, c = items[i]
            hs, ks = slice(h * depth, (h + 1) * depth), slice(c * TILE, (c + 1) * TILE)
            if c == 0:
                q, do, o = q_ref[hs, qs], do_ref[hs, qs], o_ref[hs, qs]
                centre = jnp.sum(
                    do.astype(jnp.float32) * o.astype(jnp.float32), axis=0, keepdims=True
                )
                queries.append(
                    jnp.concatenate([q, three_rows(-lse_ref[h, :, qs], base, 4)], axis=0)
                )
                grads.append(jnp.concatenate([do, three_rows(-centre, 0.0, 0)], axis=0))
            return dot(kn[h, ks, :], queries[h], NN), dot(vn[h, ks, :], grads[h], NN)

        pending = [first(i) for i in range(min(ahead, len(items)))]
        dq = None
        for i, (h, c) in enumerate(items):
            if i + ahead < len(items):
                pending.append(first(i + ahead))
            scores, dp = pending[i]
            pending[i] = None
            hs, ks = slice(h * depth, (h + 1) * depth), slice(c * TILE, (c + 1) * TILE)
            p = jnp.exp2(scores)
            ds = (p * dp).astype(LOW)
            dva[hs, ks] += dot(do_ref[hs, qs], p.astype(LOW), NT)
            dka[hs, ks] += dot(q_ref[hs, qs], ds, NT)
            part = dot(k_ref[hs, ks], ds, NN)
            dq = part if c == 0 else dq + part
            if c == n - 1:
                d_ref[0, hs, qs] = (dq * factor_ref[...]).astype(LOW)
                scale_ref[...] += dq * q_ref[hs, qs].astype(jnp.float32)

    for_each_tile(length, lambda t: counts[s, t], tile)
    d_ref[1] = (dka[...] * LN2).astype(LOW)
    d_ref[2] = dva[...].astype(LOW)


def attention_backward(qkv, context, grad_context, lse, qx, kx, counts, factor, depth, length, groups):
    heads = HEADS_PER_STEP
    seqs = qkv.shape[2] // length
    group = heads * depth
    start, step, count = groups

    def at(h):
        return start + h * step

    def third(i):
        return pl.BlockSpec((None, group, length), lambda h, s, counts: (i, at(h), s))

    whole = pl.BlockSpec((group, length), lambda h, s, counts: (at(h), s))
    extra = pl.BlockSpec((EXTRA, length), lambda h, s, counts: (0, s))
    return pl.pallas_call(
        functools.partial(attention_backward_kernel, heads, depth, length, 1),
        grid_spec=pltpu.PrefetchScalarGridSpec(
            num_scalar_prefetch=1,
            grid=(count, seqs),
            in_specs=[
                third(0),
                third(1),
                third(2),
                whole,
                whole,
                pl.BlockSpec((heads, 1, length), lambda h, s, counts: (at(h), 0, s)),
                extra,
                extra,
                pl.BlockSpec((depth, TILE), lambda h, s, counts: (0, 0)),
            ],
            out_specs=[
                pl.BlockSpec((3, group, length), lambda h, s, counts: (0, h, s)),
                pl.BlockSpec((depth, TILE), lambda h, s, counts: (0, 0)),
            ],
            scratch_shapes=[
                pltpu.VMEM((heads, length, depth + EXTRA), LOW),
                pltpu.VMEM((heads, length, depth + EXTRA), LOW),
                pltpu.VMEM((group, length), jnp.float32),
                pltpu.VMEM((group, length), jnp.float32),
            ],
        ),
        out_shape=[
            jax.ShapeDtypeStruct((3, count * group, seqs * length), LOW),
            jax.ShapeDtypeStruct((depth, TILE), jnp.float32),
        ],
        cost_estimate=pl.CostEstimate(
            flops=7 * count * heads * 256 * length * length * seqs,
            bytes_accessed=16 * count * group * seqs * length,
            transcendentals=count * heads * length * length * seqs,
        ),
        name="attention_backward",
    )(counts, qkv, qkv, qkv, context, grad_context, lse, qx, kx, factor)


def exchange(x, bit, n):
    return lax.ppermute(x, AXIS, [(i, i ^ bit) for i in range(n)])


def halve(x, dim, bit, n):
    mine = (lax.axis_index(AXIS) // bit) % 2
    away = lax.dynamic_index_in_dim(x, 1 - mine, dim, keepdims=False)
    keep = lax.dynamic_index_in_dim(x, mine, dim, keepdims=False)
    came = exchange(away, bit, n)
    return (keep.astype(jnp.float32) + came.astype(jnp.float32)).astype(LOW)


def planes_to_mine(x, n):
    x = halve(x, 4, 1, n)
    half = x.shape[-1] // 2
    left, right = x[..., :half], x[..., half:]
    left = halve(left, 3, 2, n)
    right = halve(right, 2, 4, n)
    left = halve(left, 2, 4, n)
    right = halve(right, 2, 2, n)
    return jnp.concatenate([left, right], axis=-1)


def scatter_all(parts, n):
    if n != 32:
        return lax.psum_scatter(jnp.stack(parts), AXIS, scatter_dimension=1, tiled=True)
    rows, width = parts[0].shape
    x = jnp.stack([p.astype(LOW) for p in parts])
    x = x.reshape(len(parts), 4, 2, 2, 2, rows // n, width)
    x = planes_to_mine(x, n)
    x = halve(x.reshape(len(parts), 2, 2, rows // n, width), 1, 16, n)
    return halve(x, 1, 8, n).astype(jnp.float32)


def scatter_half(x, parity, n):
    three, heads, depth, width = x.shape
    x = x.astype(LOW).reshape(three, 2, 2, 2, 2, depth // 2, width)
    x = planes_to_mine(x, n)
    x = halve(x, 1, 16, n)
    senders = [(i, i ^ 8) for i in range(n) if (i // 8) % 2 != parity]
    return x.astype(jnp.float32) + lax.ppermute(x, AXIS, senders).astype(jnp.float32)


def sum_all(x, n):
    if n & (n - 1):
        return lax.psum(x, AXIS)
    bit = 1
    while bit < n:
        x = x + exchange(x, bit, n)
        bit *= 2
    return x


def on_device(n, *arguments):
    (
        inputs,
        block_ids,
        cotangent,
        first_gain,
        query_weight,
        key_weight,
        value_weight,
        output_weight,
        second_gain,
        up_weight,
        down_weight,
        query_scale,
    ) = arguments
    seqs, length, width = inputs.shape
    tokens = seqs * length
    depth = query_scale.shape[0]
    shard = first_gain.shape[0]
    me = lax.axis_index(AXIS)

    gains = lax.all_gather(
        jnp.stack([first_gain, second_gain]).astype(jnp.float32), AXIS, axis=1, tiled=True
    )
    wide = jnp.stack([query_weight.T, key_weight.T, value_weight.T])
    qkv_weight = lax.all_gather(wide, AXIS, axis=1, tiled=True).reshape(3 * width, width)
    late = jnp.stack([output_weight.T, up_weight.T, down_weight.T])
    late = lax.all_gather(late, AXIS, axis=1, tiled=True)
    output_t, up_t, down_t = late[0], late[1], late[2]

    ids = block_ids.reshape(1, tokens)
    row = lax.broadcasted_iota(jnp.int32, (EXTRA, tokens), 0)
    qx = ((ids == row) & (row < BLOCKS)).astype(LOW)
    kx = jnp.where(
        row < BLOCKS, jnp.where(ids > row, -1e30, 0.0), jnp.where(row < BLOCKS + 3, 1.0, 0.0)
    ).astype(LOW)
    last = block_ids[:, TILE - 1 :: TILE]
    seen = jnp.sum(block_ids[:, None, :] <= last[:, :, None], axis=-1)
    counts = ((seen + TILE - 1) // TILE).astype(jnp.int32)

    x = inputs.reshape(tokens, width).astype(jnp.float32)
    g = cotangent.reshape(tokens, width)
    root1 = lax.rsqrt(jnp.mean(x * x, axis=-1, keepdims=True) + EPSILON)
    normed = (x * root1 * gains[0]).astype(LOW)
    factor = query_scale / math.sqrt(depth)
    heads = width // depth
    row_scale = jnp.concatenate(
        [jnp.tile(factor * LOG2E, heads), jnp.ones((2 * width,), jnp.float32)]
    )
    qkv = (dot(qkv_weight, normed, NT) * row_scale[:, None]).astype(LOW)
    qkv = qkv.reshape(3, width, tokens)
    context, lse = attention_forward(qkv, qx, kx, counts, depth, length)
    hidden = x + dot(context, output_t, TT)
    root2 = lax.rsqrt(jnp.mean(hidden * hidden, axis=-1, keepdims=True) + EPSILON)
    normed2 = (hidden * root2 * gains[1]).astype(LOW)
    upward = dot(normed2, up_t, NT)
    s = jax.nn.sigmoid(upward)
    activated = (upward * s).astype(LOW)
    output = (hidden + dot(activated, down_t, NT)).astype(LOW)

    grad_down = dot(g, activated, TN)
    grad_activated = dot(g, down_t, NN)
    grad_upward = (grad_activated * s * (1.0 + upward * (1.0 - s))).astype(LOW)
    grad_up = dot(grad_upward, normed2, TN)
    grad_normed2 = dot(grad_upward, up_t, NN)
    grad_gain2 = jnp.sum(grad_normed2 * hidden * root2, axis=0)
    w = grad_normed2 * gains[1]
    grad_hidden = (
        g.astype(jnp.float32)
        + root2 * w
        - hidden * (root2 * root2 * root2) * jnp.mean(w * hidden, axis=-1, keepdims=True)
    )
    grad_branch = grad_hidden.astype(LOW)
    grad_output = dot(grad_branch, context, (((0,), (1,)), ((), ())))
    grad_context = dot(output_t, grad_branch, TT).astype(LOW)
    late_grads = scatter_all([grad_output, grad_up, grad_down], n)

    factor_rows = jnp.broadcast_to(factor[:, None], (depth, TILE))
    pairs = []
    for parity in range(2):
        pairs.append(
            attention_backward(
                qkv, context, grad_context, lse, qx, kx, counts, factor_rows, depth, length,
                (parity, 2, heads // HEADS_PER_STEP // 2),
            )
        )
    scale_part = jnp.sum(pairs[0][1] + pairs[1][1], axis=1) / (factor * LOG2E) / math.sqrt(depth)
    weight_parts = [
        dot(d.reshape(-1, tokens), normed, NN).reshape(3, heads // 2, depth, width)
        for d, _ in pairs
    ]
    if n == 32:
        own = (me // 8) % 2
        halves = [scatter_half(part, parity, n) for parity, part in enumerate(weight_parts)]
        early_grads = jnp.where(own == 0, halves[0], halves[1])
    else:
        both = [p.reshape(3, 2, 1, -1, width) for p in weight_parts]
        both = jnp.concatenate(both, axis=2).reshape(3, width, width)
        early_grads = lax.psum_scatter(both, AXIS, scatter_dimension=1, tiled=True)

    weight = qkv_weight.reshape(3, 2, 2, -1, width)
    grad_normed = sum(
        dot(d.reshape(-1, tokens), weight[:, :, parity].reshape(-1, width), TN)
        for parity, (d, _) in enumerate(pairs)
    )
    grad_gain1 = jnp.sum(grad_normed * x * root1, axis=0)
    w = grad_normed * gains[0]
    grad_inputs = (
        grad_hidden
        + root1 * w
        - x * (root1 * root1 * root1) * jnp.mean(w * x, axis=-1, keepdims=True)
    )
    small = jnp.concatenate([grad_gain1, grad_gain2, scale_part])
    small = sum_all(small, n)
    gain1 = lax.dynamic_slice_in_dim(small, me * shard, shard)
    gain2 = lax.dynamic_slice_in_dim(small, width + me * shard, shard)
    scale_total = small[2 * width :]

    return (
        output.reshape(seqs, length, width),
        grad_inputs.reshape(seqs, length, width),
        gain1,
        early_grads[0].T,
        early_grads[1].T,
        early_grads[2].T,
        late_grads[0].T,
        gain2,
        late_grads[1].T,
        late_grads[2].T,
        scale_total,
    )


def solution(mesh):
    rows, columns = P(AXIS), P(None, AXIS)
    in_specs = (rows, rows, rows, rows, *[columns] * 4, rows, columns, columns, P())
    out_specs = (rows, rows, rows, *[columns] * 4, rows, columns, columns, P())
    return jax.shard_map(
        functools.partial(on_device, mesh.shape[AXIS]),
        mesh=mesh,
        in_specs=in_specs,
        out_specs=out_specs,
        check_vma=False,
    )
```

```python
import functools
import math

import jax
import jax.numpy as jnp
from jax import lax
from jax.experimental import pallas as pl
from jax.experimental.pallas import tpu as pltpu
from jax.sharding import PartitionSpec as P

EPSILON = 1e-06
AXIS = "fsdp"
BLOCKS = 4
TILE = 256
EXTRA = 16
HEADS_PER_STEP = 4
LOW = jnp.bfloat16
LOG2E = math.log2(math.e)
LN2 = math.log(2.0)
NN = (((1,), (0,)), ((), ()))
NT = (((1,), (1,)), ((), ()))
TN = (((0,), (0,)), ((), ()))
TT = (((0,), (1,)), ((), ()))


def dot(left, right, dims):
    return lax.dot_general(left, right, dims, preferred_element_type=jnp.float32)


def three_rows(value, base, at):
    row = lax.broadcasted_iota(jnp.int32, (EXTRA, value.shape[1]), 0)
    first = value.astype(LOW).astype(jnp.float32)
    rest = value - first
    second = rest.astype(LOW).astype(jnp.float32)
    third = rest - second
    rows = jnp.where(row == at + 1, second, jnp.where(row == at + 2, third, base))
    return jnp.where(row == at, first, rows).astype(LOW)


def fold(x, op):
    return op(x.reshape(x.shape[0] // 8, 8, x.shape[1]), axis=0)


def for_each_tile(length, count_of, body):
    @pl.loop(0, length // TILE)
    def _(t):
        count = count_of(t)
        for n in range(1, length // TILE + 1):

            @pl.when(count == n)
            def _(n=n):
                body(pl.ds(pl.multiple_of(t * TILE, TILE), TILE), n)


def attention_forward_kernel(
    heads, depth, length, counts, q_ref, k_ref, v_ref, qx_ref, kx_ref, o_ref, lse_ref, kn, sb
):
    s = pl.program_id(1)
    for h in range(heads):
        kn[h] = jnp.concatenate([k_ref[h * depth : (h + 1) * depth, :], kx_ref[...]], axis=0).T

    def tile(qs, n):
        qx = qx_ref[:, qs]
        peaks = [None] * (heads + 1)
        for h in range(heads + 1):
            out = total = None
            if h > 0:
                peak = jnp.max(peaks[h - 1], axis=0, keepdims=True)
            for c in range(n):
                ks = slice(c * TILE, (c + 1) * TILE)
                if h < heads:
                    q = jnp.concatenate([q_ref[h * depth : (h + 1) * depth, qs], qx], axis=0)
                    scores = dot(kn[h, ks, :], q, NN)
                    sb[h % 2, ks, :] = scores
                    part = fold(scores, jnp.max)
                    peaks[h] = part if c == 0 else jnp.maximum(peaks[h], part)
                if h > 0:
                    p = jnp.exp2(sb[(h - 1) % 2, ks, :] - peak)
                    part = fold(p, jnp.sum)
                    total = part if c == 0 else total + part
                    part = dot(v_ref[(h - 1) * depth : h * depth, ks], p.astype(LOW), NN)
                    out = part if c == 0 else out + part
            if h > 0:
                total = jnp.sum(total, axis=0, keepdims=True)
                o_ref[(h - 1) * depth : h * depth, qs] = (out * (1.0 / total)).astype(LOW)
                lse_ref[h - 1, :, qs] = peak + jnp.log2(total)

    for_each_tile(length, lambda t: counts[s, t], tile)


def attention_forward(qkv, qx, kx, counts, depth, length):
    heads = HEADS_PER_STEP
    rows = qkv.shape[1]
    head_count, seqs = rows // depth, qkv.shape[2] // length
    group = heads * depth

    def third(i):
        return pl.BlockSpec((None, group, length), lambda h, s, counts: (i, h, s))

    extra = pl.BlockSpec((EXTRA, length), lambda h, s, counts: (0, s))
    return pl.pallas_call(
        functools.partial(attention_forward_kernel, heads, depth, length),
        grid_spec=pltpu.PrefetchScalarGridSpec(
            num_scalar_prefetch=1,
            grid=(head_count // heads, seqs),
            in_specs=[third(0), third(1), third(2), extra, extra],
            out_specs=[
                pl.BlockSpec((group, length), lambda h, s, counts: (h, s)),
                pl.BlockSpec((heads, 1, length), lambda h, s, counts: (h, 0, s)),
            ],
            scratch_shapes=[
                pltpu.VMEM((heads, length, depth + EXTRA), LOW),
                pltpu.VMEM((2, length, TILE), jnp.float32),
            ],
        ),
        out_shape=[
            jax.ShapeDtypeStruct((rows, seqs * length), LOW),
            jax.ShapeDtypeStruct((head_count, 1, seqs * length), jnp.float32),
        ],
        cost_estimate=pl.CostEstimate(
            flops=4 * head_count * 256 * length * length * seqs,
            bytes_accessed=8 * rows * seqs * length,
            transcendentals=head_count * length * length * seqs,
        ),
        name="attention_forward",
    )(counts, qkv, qkv, qkv, qx, kx)


def attention_backward_kernel(
    heads,
    depth,
    length,
    ahead,
    counts,
    q_ref,
    k_ref,
    v_ref,
    o_ref,
    do_ref,
    lse_ref,
    qx_ref,
    kx_ref,
    factor_ref,
    d_ref,
    scale_ref,
    kn,
    vn,
    dka,
    dva,
):
    s = pl.program_id(1)

    @pl.when((pl.program_id(0) == 0) & (s == 0))
    def _():
        scale_ref[...] = jnp.zeros_like(scale_ref)

    dka[...] = jnp.zeros_like(dka)
    dva[...] = jnp.zeros_like(dva)
    ones = jnp.where(lax.broadcasted_iota(jnp.int32, (EXTRA, length), 0) < 3, 1.0, 0.0).astype(LOW)
    for h in range(heads):
        hs = slice(h * depth, (h + 1) * depth)
        kn[h] = jnp.concatenate([k_ref[hs, :], kx_ref[...]], axis=0).T
        vn[h] = jnp.concatenate([v_ref[hs, :], ones], axis=0).T

    def tile(qs, n):
        base = qx_ref[:, qs].astype(jnp.float32)
        queries, grads = [], []
        items = [(h, c) for h in range(heads) for c in range(n)]

        def first(i):
            h, c = items[i]
            hs, ks = slice(h * depth, (h + 1) * depth), slice(c * TILE, (c + 1) * TILE)
            if c == 0:
                q, do, o = q_ref[hs, qs], do_ref[hs, qs], o_ref[hs, qs]
                centre = jnp.sum(
                    do.astype(jnp.float32) * o.astype(jnp.float32), axis=0, keepdims=True
                )
                queries.append(
                    jnp.concatenate([q, three_rows(-lse_ref[h, :, qs], base, 4)], axis=0)
                )
                grads.append(jnp.concatenate([do, three_rows(-centre, 0.0, 0)], axis=0))
            return dot(kn[h, ks, :], queries[h], NN), dot(vn[h, ks, :], grads[h], NN)

        pending = [first(i) for i in range(min(ahead, len(items)))]
        dq = None
        for i, (h, c) in enumerate(items):
            if i + ahead < len(items):
                pending.append(first(i + ahead))
            scores, dp = pending[i]
            pending[i] = None
            hs, ks = slice(h * depth, (h + 1) * depth), slice(c * TILE, (c + 1) * TILE)
            p = jnp.exp2(scores)
            ds = (p * dp).astype(LOW)
            dva[hs, ks] += dot(do_ref[hs, qs], p.astype(LOW), NT)
            dka[hs, ks] += dot(q_ref[hs, qs], ds, NT)
            part = dot(k_ref[hs, ks], ds, NN)
            dq = part if c == 0 else dq + part
            if c == n - 1:
                d_ref[0, hs, qs] = (dq * factor_ref[...]).astype(LOW)
                scale_ref[...] += dq * q_ref[hs, qs].astype(jnp.float32)

    for_each_tile(length, lambda t: counts[s, t], tile)
    d_ref[1] = (dka[...] * LN2).astype(LOW)
    d_ref[2] = dva[...].astype(LOW)


def attention_backward(qkv, context, grad_context, lse, qx, kx, counts, factor, depth, length, groups):
    heads = HEADS_PER_STEP
    seqs = qkv.shape[2] // length
    group = heads * depth
    start, step, count = groups

    def at(h):
        return start + h * step

    def third(i):
        return pl.BlockSpec((None, group, length), lambda h, s, counts: (i, at(h), s))

    whole = pl.BlockSpec((group, length), lambda h, s, counts: (at(h), s))
    extra = pl.BlockSpec((EXTRA, length), lambda h, s, counts: (0, s))
    return pl.pallas_call(
        functools.partial(attention_backward_kernel, heads, depth, length, 1),
        grid_spec=pltpu.PrefetchScalarGridSpec(
            num_scalar_prefetch=1,
            grid=(count, seqs),
            in_specs=[
                third(0),
                third(1),
                third(2),
                whole,
                whole,
                pl.BlockSpec((heads, 1, length), lambda h, s, counts: (at(h), 0, s)),
                extra,
                extra,
                pl.BlockSpec((depth, TILE), lambda h, s, counts: (0, 0)),
            ],
            out_specs=[
                pl.BlockSpec((3, group, length), lambda h, s, counts: (0, h, s)),
                pl.BlockSpec((depth, TILE), lambda h, s, counts: (0, 0)),
            ],
            scratch_shapes=[
                pltpu.VMEM((heads, length, depth + EXTRA), LOW),
                pltpu.VMEM((heads, length, depth + EXTRA), LOW),
                pltpu.VMEM((group, length), jnp.float32),
                pltpu.VMEM((group, length), jnp.float32),
            ],
        ),
        out_shape=[
            jax.ShapeDtypeStruct((3, count * group, seqs * length), LOW),
            jax.ShapeDtypeStruct((depth, TILE), jnp.float32),
        ],
        cost_estimate=pl.CostEstimate(
            flops=7 * count * heads * 256 * length * length * seqs,
            bytes_accessed=16 * count * group * seqs * length,
            transcendentals=count * heads * length * length * seqs,
        ),
        name="attention_backward",
    )(counts, qkv, qkv, qkv, context, grad_context, lse, qx, kx, factor)


def mean_rows(x):
    return jnp.mean(x, axis=-1, keepdims=True)


def front_kernel(x_ref, gain_ref, factor_ref, w_ref, normed_ref, qkv_ref):
    x = x_ref[...].astype(jnp.float32)
    normed = (x * lax.rsqrt(mean_rows(x * x) + EPSILON) * gain_ref[...]).astype(LOW)
    normed_ref[...] = normed
    for i in range(3):
        y = dot(w_ref[i], normed, NT)
        if i == 0:
            y = y * jnp.concatenate([factor_ref[...]] * (y.shape[1] // 128), axis=1)
        qkv_ref[i] = y.astype(LOW)


def front(x, gain, factor_rows, weight):
    tokens, width = x.shape
    rows = weight.shape[1]
    return pl.pallas_call(
        front_kernel,
        grid=(tokens // TILE,),
        in_specs=[
            pl.BlockSpec((TILE, width), lambda i: (i, 0)),
            pl.BlockSpec((1, width), lambda i: (0, 0)),
            pl.BlockSpec((rows, 128), lambda i: (0, 0)),
            pl.BlockSpec((3, rows, width), lambda i: (0, 0, 0)),
        ],
        out_specs=[
            pl.BlockSpec((TILE, width), lambda i: (i, 0)),
            pl.BlockSpec((3, rows, TILE), lambda i: (0, 0, i)),
        ],
        out_shape=[
            jax.ShapeDtypeStruct((tokens, width), LOW),
            jax.ShapeDtypeStruct((3, rows, tokens), LOW),
        ],
        cost_estimate=pl.CostEstimate(
            flops=6 * tokens * rows * width, bytes_accessed=16 * tokens * width, transcendentals=0
        ),
        name="front",
    )(x, gain, factor_rows, weight)


def middle_kernel(
    unit,
    core_ref,
    x_ref,
    context_ref,
    g_ref,
    gain_ref,
    w_ref,
    out_ref,
    grad_hidden_ref,
    grad_context_ref,
    keep_ref,
    send_ref,
    gain_grad_ref,
    total,
):
    step = pl.program_id(0)
    width = x_ref.shape[1]

    @pl.when(step == 0)
    def _():
        total[...] = jnp.zeros_like(total)
        gain_grad_ref[...] = jnp.zeros_like(gain_grad_ref)

    g = g_ref[...]
    gain = gain_ref[...]
    context = context_ref[...].T
    hidden = x_ref[...].astype(jnp.float32) + dot(context, w_ref[0], NT)
    root = lax.rsqrt(mean_rows(hidden * hidden) + EPSILON)
    scaled = hidden * root
    normed = (scaled * gain).astype(LOW)
    upward = dot(normed, w_ref[1], NT)
    s = jax.nn.sigmoid(upward)
    activated = (upward * s).astype(LOW)
    out_ref[...] = (hidden + dot(activated, w_ref[2], NT)).astype(LOW)
    slope = s * (1.0 + upward * (1.0 - s))
    grad_upward = (dot(g, w_ref[2], NN) * slope).astype(LOW)
    total[2] += dot(g.T, activated, NN)
    grad_normed = dot(grad_upward, w_ref[1], NN)
    total[1] += dot(grad_upward.T, normed, NN)
    gain_grad_ref[...] += fold(grad_normed * scaled, jnp.sum)
    w = grad_normed * gain
    grad_hidden = g.astype(jnp.float32) + root * (w - scaled * mean_rows(w * scaled))
    grad_hidden_ref[...] = grad_hidden
    branch = grad_hidden.astype(LOW)
    grad_context_ref[...] = dot(branch, w_ref[0], NN).astype(LOW).T
    total[0] += dot(branch.T, context, NN)

    @pl.when(step == pl.num_programs(0) - 1)
    def _():
        core = core_ref[0]

        @pl.loop(0, width // (2 * unit))
        def _(j):
            for i in range(3):
                at = pl.multiple_of((2 * j + core) * unit, 8)
                keep_ref[i, j] = total[i, pl.ds(at, unit), :].astype(LOW)
                at = pl.multiple_of((2 * j + 1 - core) * unit, 8)
                send_ref[i, j] = total[i, pl.ds(at, unit), :].astype(LOW)


def middle(core, x, context, g, gain, weight, unit):
    tokens, width = x.shape
    chips = width // (2 * unit)
    rows = pl.BlockSpec((TILE, width), lambda i, core: (i, 0))
    columns = pl.BlockSpec((width, TILE), lambda i, core: (0, i))
    once = pl.Buffered(1)
    half = pl.BlockSpec((3, chips, unit, width), lambda i, core: (0, 0, 0, 0), pipeline_mode=once)
    return pl.pallas_call(
        functools.partial(middle_kernel, unit),
        grid_spec=pltpu.PrefetchScalarGridSpec(
            num_scalar_prefetch=1,
            grid=(tokens // TILE,),
            in_specs=[
                rows,
                columns,
                rows,
                pl.BlockSpec((1, width), lambda i, core: (0, 0)),
                pl.BlockSpec((3, width, width), lambda i, core: (0, 0, 0), pipeline_mode=once),
            ],
            out_specs=[
                rows,
                rows,
                columns,
                half,
                half,
                pl.BlockSpec((8, width), lambda i, core: (0, 0)),
            ],
            scratch_shapes=[pltpu.VMEM((3, width, width), jnp.float32)],
        ),
        out_shape=[
            jax.ShapeDtypeStruct((tokens, width), LOW),
            jax.ShapeDtypeStruct((tokens, width), jnp.float32),
            jax.ShapeDtypeStruct((width, tokens), LOW),
            jax.ShapeDtypeStruct((3, chips, unit, width), LOW),
            jax.ShapeDtypeStruct((3, chips, unit, width), LOW),
            jax.ShapeDtypeStruct((8, width), jnp.float32),
        ],
        compiler_params=pltpu.CompilerParams(vmem_limit_bytes=66_000_000),
        cost_estimate=pl.CostEstimate(
            flops=18 * tokens * width * width,
            bytes_accessed=14 * tokens * width + 12 * width * width,
            transcendentals=tokens * width,
        ),
        name="middle",
    )(core, x, context, g, gain, weight)


def back_kernel(x_ref, grad_hidden_ref, gain_ref, w_ref, *rest):
    *d_refs, out_ref, gain_grad_ref = rest
    groups = len(d_refs)
    rows = d_refs[0].shape[1]

    @pl.when(pl.program_id(0) == 0)
    def _():
        gain_grad_ref[...] = jnp.zeros_like(gain_grad_ref)

    x = x_ref[...].astype(jnp.float32)
    root = lax.rsqrt(mean_rows(x * x) + EPSILON)
    scaled = x * root
    parts = [
        d_refs[p][i].T for i in range(3) for p in range(groups)
    ]
    grad_normed = dot(jnp.concatenate(parts, axis=1), w_ref[...], NN)
    gain_grad_ref[...] += fold(grad_normed * scaled, jnp.sum)
    w = grad_normed * gain_ref[...]
    out_ref[...] = grad_hidden_ref[...] + root * (w - scaled * mean_rows(w * scaled))


def back(x, grad_hidden, gain, weight, grads):
    tokens, width = x.shape
    rows = pl.BlockSpec((TILE, width), lambda i: (i, 0))
    group = grads[0].shape[1]
    return pl.pallas_call(
        back_kernel,
        grid=(tokens // TILE,),
        in_specs=[
            rows,
            rows,
            pl.BlockSpec((1, width), lambda i: (0, 0)),
            pl.BlockSpec(weight.shape, lambda i: (0, 0)),
        ]
        + [pl.BlockSpec((3, group, TILE), lambda i: (0, 0, i))] * len(grads),
        out_specs=[rows, pl.BlockSpec((8, width), lambda i: (0, 0))],
        out_shape=[
            jax.ShapeDtypeStruct((tokens, width), jnp.float32),
            jax.ShapeDtypeStruct((8, width), jnp.float32),
        ],
        cost_estimate=pl.CostEstimate(
            flops=6 * tokens * width * width, bytes_accessed=18 * tokens * width, transcendentals=0
        ),
        name="back",
    )(x, grad_hidden, gain, weight, *grads)


def exchange(x, bit, n):
    return lax.ppermute(x, AXIS, [(i, i ^ bit) for i in range(n)])


def tie(*values):
    return lax.optimization_barrier(values)


def pick(x, dim, bit):
    mine = (lax.axis_index(AXIS) // bit) % 2
    return (
        lax.dynamic_index_in_dim(x, mine, dim, keepdims=False),
        lax.dynamic_index_in_dim(x, 1 - mine, dim, keepdims=False),
    )


def plus(keep, came):
    return (keep.astype(jnp.float32) + came.astype(jnp.float32)).astype(LOW)


class Scatter:
    def __init__(self, keep, send, planes, n):
        self.n = n
        self.planes = planes
        self.keep = [keep]
        self.came = [exchange(send, 1, n)]
        self.steps = iter([self.first, self.second, self.far, self.near])

    def tie(self, *values):
        count = len(self.came)
        tied = tie(*self.came, *values)
        self.came = list(tied[:count])
        return tied[count:]

    def step(self):
        sums = [plus(k, c) for k, c in zip(self.keep, self.came)]
        next(self.steps)(*sums)

    def send(self, *pairs):
        self.keep = [keep for keep, _, _ in pairs]
        self.came = [exchange(away, bit, self.n) for _, away, bit in pairs]

    def first(self, x):
        half = x.shape[-1] // 2
        self.send((*pick(x[..., :half], 3, 2), 2), (*pick(x[..., half:], 2, 4), 4))

    def second(self, left, right):
        self.send((*pick(left, 2, 4), 4), (*pick(right, 2, 2), 2))

    def far(self, left, right):
        x = jnp.concatenate([left, right], axis=-1)
        x = x.reshape(x.shape[0], 2, -1, *x.shape[2:])
        self.send((*pick(x, 1, 16), 16))

    def near(self, x):
        if self.planes is None:
            self.send((*pick(x, 1, 8), 8))
        else:
            x = x[:, 0]
            senders = [(i, i ^ 8) for i in range(self.n) if (i // 8) % 2 != self.planes]
            self.keep, self.came = [x], [lax.ppermute(x, AXIS, senders)]

    def result(self):
        return self.keep[0].astype(jnp.float32) + self.came[0].astype(jnp.float32)


def sum_all(x, n):
    if n & (n - 1):
        return lax.psum(x, AXIS)
    bit = 1
    while bit < n:
        x = x + exchange(x, bit, n)
        bit *= 2
    return x


def on_device(n, *arguments):
    (
        inputs,
        block_ids,
        cotangent,
        first_gain,
        query_weight,
        key_weight,
        value_weight,
        output_weight,
        second_gain,
        up_weight,
        down_weight,
        query_scale,
    ) = arguments
    seqs, length, width = inputs.shape
    tokens = seqs * length
    depth = query_scale.shape[0]
    shard = first_gain.shape[0]
    me = lax.axis_index(AXIS)

    gains = lax.all_gather(
        jnp.stack([first_gain, second_gain]).astype(jnp.float32), AXIS, axis=1, tiled=True
    )
    wide = jnp.stack([query_weight.T, key_weight.T, value_weight.T])
    early = lax.all_gather(wide, AXIS, axis=1, tiled=True)
    late = jnp.stack([output_weight.T, up_weight.T, down_weight.T])
    late = lax.all_gather(late, AXIS, axis=1, tiled=True)

    ids = block_ids.reshape(1, tokens)
    row = lax.broadcasted_iota(jnp.int32, (EXTRA, tokens), 0)
    qx = ((ids == row) & (row < BLOCKS)).astype(LOW)
    kx = jnp.where(
        row < BLOCKS, jnp.where(ids > row, -1e30, 0.0), jnp.where(row < BLOCKS + 3, 1.0, 0.0)
    ).astype(LOW)
    last = block_ids[:, TILE - 1 :: TILE]
    seen = jnp.sum(block_ids[:, None, :] <= last[:, :, None], axis=-1)
    counts = ((seen + TILE - 1) // TILE).astype(jnp.int32)

    x = inputs.reshape(tokens, width)
    g = cotangent.reshape(tokens, width)
    factor = query_scale / math.sqrt(depth)
    heads = width // depth
    factor_rows = jnp.broadcast_to(factor[:, None], (depth, TILE))
    row_scale = jnp.broadcast_to(jnp.tile(factor * LOG2E, heads)[:, None], (width, 128))
    normed, qkv = front(x, gains[:1], row_scale, early)
    context, lse = attention_forward(qkv, qx, kx, counts, depth, length)
    core = (me % 2).reshape(1)
    unit = depth // 2
    output, grad_hidden, grad_context, keep, send, gain2_rows = middle(
        core, x, context, g, gains[1:], late, unit
    )

    def spatial(x, planes):
        return x.reshape(3, planes, 2, 2, unit, width)

    def backward(plane, grad_context):
        return attention_backward(
            qkv, context, grad_context, lse, qx, kx, counts, factor_rows, depth, length,
            (plane, 1, 1),
        )

    def weight_grads(*parts):
        rows = [
            dot(d.reshape(-1, tokens), normed, NN).astype(LOW).reshape(3, -1, 2, unit, width)
            for d in parts
        ]
        rows = [pick(r, 2, 1) for r in rows]
        return [jnp.concatenate([r[i] for r in rows], axis=1) for i in range(2)]

    grads = [None] * 4
    if n == 32:
        send, grad_context = tie(send, grad_context)
        late_sum = Scatter(spatial(keep, 4), spatial(send, 4), None, n)
        grads[0], part0 = backward(0, grad_context)
        (grads[0],) = late_sum.tie(grads[0])
        late_sum.step()
        *late_sum.keep, grad_context, d0 = tie(*late_sum.keep, grad_context, grads[0])
        grads[2], part2 = backward(2, grad_context)
        keep, send = weight_grads(d0, grads[2])
        even_sum = Scatter(spatial(keep, 2), spatial(send, 2), 0, n)
        keep, grad_context = tie(keep, grad_context)
        even_sum.keep = [spatial(keep, 2)]
        grads[1], part1 = backward(1, grad_context)
        (grads[1],) = late_sum.tie(grads[1])
        late_sum.step()
        (d1,) = even_sum.tie(grads[1])
        even_sum.step()
        *even_sum.keep, k0, k1, grad_context = tie(*even_sum.keep, *late_sum.keep, grad_context)
        late_sum.keep = [k0, k1]
        grads[3], part3 = backward(3, grad_context)
        (d3,) = late_sum.tie(grads[3])
        late_sum.step()
        (d3,) = even_sum.tie(d3)
        even_sum.step()
        keep, send = weight_grads(d1, d3)
        odd_sum = Scatter(spatial(keep, 2), spatial(send, 2), 1, n)
        *late_sum.keep, keep, d3 = tie(*late_sum.keep, keep, d3)
        odd_sum.keep = [spatial(keep, 2)]
        grads[3] = d3
    else:
        parts = [backward(p, grad_context) for p in range(4)]
        grads = [d for d, _ in parts]
        part0, part1, part2, part3 = [part for _, part in parts]
        mine = me % 2 == 0
        even, odd = jnp.where(mine, keep, send), jnp.where(mine, send, keep)
        both = jnp.stack([even, odd], axis=2).reshape(3, width, width).astype(jnp.float32)
        late_grads = lax.psum_scatter(both, AXIS, scatter_dimension=1, tiled=True)
        rows = [dot(d.reshape(-1, tokens), normed, NN).reshape(3, -1, width) for d in grads]
        both = jnp.concatenate(rows, axis=1)
        early_grads = lax.psum_scatter(both, AXIS, scatter_dimension=1, tiled=True)

    grad_inputs, gain1_rows = back(x, grad_hidden, gains[:1], early.reshape(-1, width), grads)
    if n == 32:
        (grad_inputs,) = odd_sum.tie(grad_inputs)
        odd_sum.step()
        (grad_inputs,) = even_sum.tie(grad_inputs)
        even_sum.step()
        late_sum.step()
        odd_sum.step()
        even_sum.step()
        late_grads = late_sum.result()
        odd_sum.step()
        odd_sum.step()
        early_grads = jnp.where((me // 8) % 2 == 0, even_sum.result(), odd_sum.result())
    scale_part = jnp.sum(part0 + part1 + part2 + part3, axis=1)
    scale_part = scale_part / (factor * LOG2E) / math.sqrt(depth)
    grad_gain1, grad_gain2 = jnp.sum(gain1_rows, axis=0), jnp.sum(gain2_rows, axis=0)
    small = jnp.concatenate([grad_gain1, grad_gain2, scale_part])
    small = sum_all(small, n)
    gain1 = lax.dynamic_slice_in_dim(small, me * shard, shard)
    gain2 = lax.dynamic_slice_in_dim(small, width + me * shard, shard)
    scale_total = small[2 * width :]

    return (
        output.reshape(seqs, length, width),
        grad_inputs.reshape(seqs, length, width),
        gain1,
        early_grads[0].T,
        early_grads[1].T,
        early_grads[2].T,
        late_grads[0].T,
        gain2,
        late_grads[1].T,
        late_grads[2].T,
        scale_total,
    )


def solution(mesh):
    rows, columns = P(AXIS), P(None, AXIS)
    in_specs = (rows, rows, rows, rows, *[columns] * 4, rows, columns, columns, P())
    out_specs = (rows, rows, rows, *[columns] * 4, rows, columns, columns, P())
    return jax.shard_map(
        functools.partial(on_device, mesh.shape[AXIS]),
        mesh=mesh,
        in_specs=in_specs,
        out_specs=out_specs,
        check_vma=False,
    )
```

```python
import functools
import math

import jax
import jax.numpy as jnp
from jax import lax
from jax.experimental import pallas as pl
from jax.experimental.pallas import tpu as pltpu
from jax.sharding import PartitionSpec as P

EPSILON = 1e-06
AXIS = "fsdp"
BLOCKS = 4
TILE = 256
EXTRA = 16
HEADS_PER_STEP = 4
LOW = jnp.bfloat16
LOG2E = math.log2(math.e)
LN2 = math.log(2.0)
NN = (((1,), (0,)), ((), ()))
NT = (((1,), (1,)), ((), ()))
TN = (((0,), (0,)), ((), ()))
TT = (((0,), (1,)), ((), ()))


def dot(left, right, dims):
    return lax.dot_general(left, right, dims, preferred_element_type=jnp.float32)


def three_rows(value, base, at):
    row = lax.broadcasted_iota(jnp.int32, (EXTRA, value.shape[1]), 0)
    first = value.astype(LOW).astype(jnp.float32)
    rest = value - first
    second = rest.astype(LOW).astype(jnp.float32)
    third = rest - second
    rows = jnp.where(row == at + 1, second, jnp.where(row == at + 2, third, base))
    return jnp.where(row == at, first, rows).astype(LOW)


def fold(x, op):
    return op(x.reshape(x.shape[0] // 8, 8, x.shape[1]), axis=0)


def for_each_tile(length, count_of, body):
    @pl.loop(0, length // TILE)
    def _(t):
        count = count_of(t)
        for n in range(1, length // TILE + 1):

            @pl.when(count == n)
            def _(n=n):
                body(pl.ds(pl.multiple_of(t * TILE, TILE), TILE), n)


def attention_forward_kernel(
    heads, depth, length, counts, normed_ref, mine_ref, other_ref, factor_ref, qx_ref, kx_ref,
    qkv_ref, o_ref, lse_ref, kn, sb,
):
    s = pl.program_id(0)
    unit = depth // 2
    for at in range(0, length, TILE):
        normed = normed_ref[at : at + TILE, :]
        for part, w_ref in enumerate((mine_ref, other_ref)):
            y = dot(w_ref[...], normed, NT)
            for h in range(heads):
                for i in range(3):
                    rows = y[(3 * h + i) * unit : (3 * h + i + 1) * unit]
                    if i == 0:
                        rows = rows * factor_ref[part * unit : (part + 1) * unit, :]
                    start = h * depth + part * unit
                    qkv_ref[i, start : start + unit, at : at + TILE] = rows.astype(LOW)
    q_ref, k_ref, v_ref = qkv_ref.at[0], qkv_ref.at[1], qkv_ref.at[2]
    for h in range(heads):
        kn[h] = jnp.concatenate([k_ref[h * depth : (h + 1) * depth, :], kx_ref[...]], axis=0).T

    def tile(qs, n):
        qx = qx_ref[:, qs]
        peaks = [None] * (heads + 1)
        for h in range(heads + 1):
            out = total = None
            if h > 0:
                peak = jnp.max(peaks[h - 1], axis=0, keepdims=True)
            for c in range(n):
                ks = slice(c * TILE, (c + 1) * TILE)
                if h < heads:
                    q = jnp.concatenate([q_ref[h * depth : (h + 1) * depth, qs], qx], axis=0)
                    scores = dot(kn[h, ks, :], q, NN)
                    sb[h % 2, ks, :] = scores
                    part = fold(scores, jnp.max)
                    peaks[h] = part if c == 0 else jnp.maximum(peaks[h], part)
                if h > 0:
                    p = jnp.exp2(sb[(h - 1) % 2, ks, :] - peak)
                    part = fold(p, jnp.sum)
                    total = part if c == 0 else total + part
                    part = dot(v_ref[(h - 1) * depth : h * depth, ks], p.astype(LOW), NN)
                    out = part if c == 0 else out + part
            if h > 0:
                total = jnp.sum(total, axis=0, keepdims=True)
                o_ref[(h - 1) * depth : h * depth, qs] = (out * (1.0 / total)).astype(LOW)
                lse_ref[h - 1, :, qs] = peak + jnp.log2(total)

    for_each_tile(length, lambda t: counts[s, t], tile)


def attention_forward(normed, mine, other, factor, qx, kx, counts, depth, length):
    tokens, width = normed.shape
    seqs = tokens // length
    heads = mine.shape[0] * 2 // (3 * depth)
    group = heads * depth
    extra = pl.BlockSpec((EXTRA, length), lambda s, counts: (0, s))
    weight = pl.BlockSpec(mine.shape, lambda s, counts: (0, 0))
    return pl.pallas_call(
        functools.partial(attention_forward_kernel, heads, depth, length),
        grid_spec=pltpu.PrefetchScalarGridSpec(
            num_scalar_prefetch=1,
            grid=(seqs,),
            in_specs=[
                pl.BlockSpec((length, width), lambda s, counts: (s, 0)),
                weight,
                weight,
                pl.BlockSpec((depth, TILE), lambda s, counts: (0, 0)),
                extra,
                extra,
            ],
            out_specs=[
                pl.BlockSpec((3, group, length), lambda s, counts: (0, 0, s)),
                pl.BlockSpec((group, length), lambda s, counts: (0, s)),
                pl.BlockSpec((heads, 1, length), lambda s, counts: (0, 0, s)),
            ],
            scratch_shapes=[
                pltpu.VMEM((heads, length, depth + EXTRA), LOW),
                pltpu.VMEM((2, length, TILE), jnp.float32),
            ],
        ),
        out_shape=[
            jax.ShapeDtypeStruct((3, group, tokens), LOW),
            jax.ShapeDtypeStruct((group, tokens), LOW),
            jax.ShapeDtypeStruct((heads, 1, tokens), jnp.float32),
        ],
        cost_estimate=pl.CostEstimate(
            flops=4 * heads * 256 * length * tokens + 6 * group * tokens * width,
            bytes_accessed=2 * tokens * width + 8 * group * tokens,
            transcendentals=heads * length * tokens,
        ),
        name="attention_forward",
    )(counts, normed, mine, other, factor, qx, kx)


def attention_backward_kernel(
    heads,
    depth,
    length,
    ahead,
    counts,
    q_ref,
    k_ref,
    v_ref,
    o_ref,
    do_ref,
    lse_ref,
    qx_ref,
    kx_ref,
    factor_ref,
    d_ref,
    scale_ref,
    kn,
    vn,
    dka,
    dva,
):
    s = pl.program_id(0)
    unit = depth // 2

    @pl.when(s == 0)
    def _():
        scale_ref[...] = jnp.zeros_like(scale_ref)

    dka[...] = jnp.zeros_like(dka)
    dva[...] = jnp.zeros_like(dva)
    ones = jnp.where(lax.broadcasted_iota(jnp.int32, (EXTRA, length), 0) < 3, 1.0, 0.0).astype(LOW)
    for h in range(heads):
        hs = slice(h * depth, (h + 1) * depth)
        kn[h] = jnp.concatenate([k_ref[hs, :], kx_ref[...]], axis=0).T
        vn[h] = jnp.concatenate([v_ref[hs, :], ones], axis=0).T

    def put(h, i, columns, value):
        for part in range(2):
            start = ((part * heads + h) * 3 + i) * unit
            rows = value[part * unit : (part + 1) * unit]
            d_ref[start : start + unit, columns] = rows.astype(LOW)

    def tile(qs, n):
        base = qx_ref[:, qs].astype(jnp.float32)
        queries, grads = [], []
        items = [(h, c) for h in range(heads) for c in range(n)]

        def first(i):
            h, c = items[i]
            hs, ks = slice(h * depth, (h + 1) * depth), slice(c * TILE, (c + 1) * TILE)
            if c == 0:
                q, do, o = q_ref[hs, qs], do_ref[hs, qs], o_ref[hs, qs]
                centre = jnp.sum(
                    do.astype(jnp.float32) * o.astype(jnp.float32), axis=0, keepdims=True
                )
                queries.append(
                    jnp.concatenate([q, three_rows(-lse_ref[h, :, qs], base, 4)], axis=0)
                )
                grads.append(jnp.concatenate([do, three_rows(-centre, 0.0, 0)], axis=0))
            return dot(kn[h, ks, :], queries[h], NN), dot(vn[h, ks, :], grads[h], NN)

        pending = [first(i) for i in range(min(ahead, len(items)))]
        dq = None
        for i, (h, c) in enumerate(items):
            if i + ahead < len(items):
                pending.append(first(i + ahead))
            scores, dp = pending[i]
            pending[i] = None
            hs, ks = slice(h * depth, (h + 1) * depth), slice(c * TILE, (c + 1) * TILE)
            p = jnp.exp2(scores)
            ds = (p * dp).astype(LOW)
            dva[hs, ks] += dot(do_ref[hs, qs], p.astype(LOW), NT)
            dka[hs, ks] += dot(q_ref[hs, qs], ds, NT)
            part = dot(k_ref[hs, ks], ds, NN)
            dq = part if c == 0 else dq + part
            if c == n - 1:
                put(h, 0, qs, dq * factor_ref[...])
                scale_ref[...] += dq * q_ref[hs, qs].astype(jnp.float32)

    for_each_tile(length, lambda t: counts[s, t], tile)
    for h in range(heads):
        put(h, 1, slice(None), dka[h * depth : (h + 1) * depth, :] * LN2)
        put(h, 2, slice(None), dva[h * depth : (h + 1) * depth, :])


def attention_backward(qkv, context, grad_context, lse, qx, kx, counts, factor, depth, length):
    _, group, tokens = qkv.shape
    heads, seqs = group // depth, tokens // length

    def third(i):
        return pl.BlockSpec((None, group, length), lambda s, counts: (i, 0, s))

    whole = pl.BlockSpec((group, length), lambda s, counts: (0, s))
    extra = pl.BlockSpec((EXTRA, length), lambda s, counts: (0, s))
    fixed = pl.BlockSpec((depth, TILE), lambda s, counts: (0, 0))
    return pl.pallas_call(
        functools.partial(attention_backward_kernel, heads, depth, length, 1),
        grid_spec=pltpu.PrefetchScalarGridSpec(
            num_scalar_prefetch=1,
            grid=(seqs,),
            in_specs=[
                third(0),
                third(1),
                third(2),
                whole,
                whole,
                pl.BlockSpec((heads, 1, length), lambda s, counts: (0, 0, s)),
                extra,
                extra,
                fixed,
            ],
            out_specs=[pl.BlockSpec((3 * group, length), lambda s, counts: (0, s)), fixed],
            scratch_shapes=[
                pltpu.VMEM((heads, length, depth + EXTRA), LOW),
                pltpu.VMEM((heads, length, depth + EXTRA), LOW),
                pltpu.VMEM((group, length), jnp.float32),
                pltpu.VMEM((group, length), jnp.float32),
            ],
        ),
        out_shape=[
            jax.ShapeDtypeStruct((3 * group, tokens), LOW),
            jax.ShapeDtypeStruct((depth, TILE), jnp.float32),
        ],
        cost_estimate=pl.CostEstimate(
            flops=7 * heads * 256 * length * tokens,
            bytes_accessed=16 * group * tokens,
            transcendentals=heads * length * tokens,
        ),
        name="attention_backward",
    )(counts, qkv, qkv, qkv, context, grad_context, lse, qx, kx, factor)


def mean_rows(x):
    return jnp.mean(x, axis=-1, keepdims=True)


def middle_kernel(
    unit,
    groups,
    core_ref,
    place_ref,
    x_ref,
    g_ref,
    gain_ref,
    w_ref,
    *rest,
):
    context_refs, rest = rest[:groups], rest[groups:]
    out_ref, grad_hidden_ref, *rest = rest
    grad_context_refs, rest = rest[:groups], rest[groups:]
    keep_ref, send_ref, gain_grad_ref, total, turned = rest
    step = pl.program_id(0)
    core = core_ref[0]
    heads = place_ref.shape[0] // groups

    def pieces():
        for j in range(groups * heads):
            for part in range(2):
                at = (2 * place_ref[j] + (core + part) % 2) * unit
                start = (2 * (j % heads) + part) * unit
                yield j // heads, slice(start, start + unit), pl.ds(pl.multiple_of(at, 8), unit)

    @pl.when(step == 0)
    def _():
        total[...] = jnp.zeros_like(total)
        gain_grad_ref[...] = jnp.zeros_like(gain_grad_ref)

    g = g_ref[...]
    gain = gain_ref[...]
    for p, rows, at in pieces():
        turned[at, :] = context_refs[p][rows, :].astype(jnp.float32)
    context = turned[...].astype(LOW).T
    hidden = x_ref[...].astype(jnp.float32) + dot(context, w_ref[0], NT)
    root = lax.rsqrt(mean_rows(hidden * hidden) + EPSILON)
    scaled = hidden * root
    normed = (scaled * gain).astype(LOW)
    upward = dot(normed, w_ref[1], NT)
    s = jax.nn.sigmoid(upward)
    activated = (upward * s).astype(LOW)
    out_ref[...] = (hidden + dot(activated, w_ref[2], NT)).astype(LOW)
    slope = s * (1.0 + upward * (1.0 - s))
    grad_upward = (dot(g, w_ref[2], NN) * slope).astype(LOW)
    total[2] += dot(g.T, activated, NN)
    grad_normed = dot(grad_upward, w_ref[1], NN)
    total[1] += dot(grad_upward.T, normed, NN)
    gain_grad_ref[...] += fold(grad_normed * scaled, jnp.sum)
    w = grad_normed * gain
    grad_hidden = g.astype(jnp.float32) + root * (w - scaled * mean_rows(w * scaled))
    grad_hidden_ref[...] = grad_hidden
    branch = grad_hidden.astype(LOW)
    turned[...] = dot(branch, w_ref[0], NN).astype(LOW).T.astype(jnp.float32)
    for p, rows, at in pieces():
        grad_context_refs[p][rows, :] = turned[at, :].astype(LOW)
    total[0] += dot(branch.T, context, NN)

    @pl.when(step == pl.num_programs(0) - 1)
    def _():
        @pl.loop(0, groups * heads)
        def _(j):
            for i in range(3):
                at = pl.multiple_of((2 * place_ref[j] + core) * unit, 8)
                keep_ref[j, i] = total[i, pl.ds(at, unit), :].astype(LOW)
                at = pl.multiple_of((2 * place_ref[j] + 1 - core) * unit, 8)
                send_ref[j, i] = total[i, pl.ds(at, unit), :].astype(LOW)


def middle(core, place, x, g, gain, weight, contexts, unit):
    tokens, width = x.shape
    chips = width // (2 * unit)
    rows = pl.BlockSpec((TILE, width), lambda i, core, place: (i, 0))
    columns = [
        pl.BlockSpec((c.shape[0], TILE), lambda i, core, place: (0, i)) for c in contexts
    ]
    once = pl.Buffered(1)
    half = pl.BlockSpec(
        (chips, 3, unit, width), lambda i, core, place: (0, 0, 0, 0), pipeline_mode=once
    )
    halves = jax.ShapeDtypeStruct((chips, 3, unit, width), LOW)
    return pl.pallas_call(
        functools.partial(middle_kernel, unit, len(contexts)),
        grid_spec=pltpu.PrefetchScalarGridSpec(
            num_scalar_prefetch=2,
            grid=(tokens // TILE,),
            in_specs=[
                rows,
                rows,
                pl.BlockSpec((1, width), lambda i, core, place: (0, 0)),
                pl.BlockSpec(
                    (3, width, width), lambda i, core, place: (0, 0, 0), pipeline_mode=once
                ),
                *columns,
            ],
            out_specs=[
                rows,
                rows,
                *columns,
                half,
                half,
                pl.BlockSpec((8, width), lambda i, core, place: (0, 0)),
            ],
            scratch_shapes=[
                pltpu.VMEM((3, width, width), jnp.float32),
                pltpu.VMEM((width, TILE), jnp.float32),
            ],
        ),
        out_shape=[
            jax.ShapeDtypeStruct((tokens, width), LOW),
            jax.ShapeDtypeStruct((tokens, width), jnp.float32),
            *[jax.ShapeDtypeStruct(c.shape, LOW) for c in contexts],
            halves,
            halves,
            jax.ShapeDtypeStruct((8, width), jnp.float32),
        ],
        compiler_params=pltpu.CompilerParams(vmem_limit_bytes=66_000_000),
        cost_estimate=pl.CostEstimate(
            flops=18 * tokens * width * width,
            bytes_accessed=14 * tokens * width + 12 * width * width,
            transcendentals=tokens * width,
        ),
        name="middle",
    )(core, place, x, g, gain, weight, *contexts)


def back_kernel(groups, x_ref, grad_hidden_ref, gain_ref, *rest):
    w_refs, d_refs, (out_ref, gain_grad_ref) = rest[: 2 * groups], rest[2 * groups : -2], rest[-2:]

    @pl.when(pl.program_id(0) == 0)
    def _():
        gain_grad_ref[...] = jnp.zeros_like(gain_grad_ref)

    x = x_ref[...].astype(jnp.float32)
    root = lax.rsqrt(mean_rows(x * x) + EPSILON)
    scaled = x * root
    grad_normed = None
    for p in range(groups):
        d = d_refs[p][...].T
        rows = d.shape[1] // 2
        for i in range(2):
            part = dot(d[:, i * rows : (i + 1) * rows], w_refs[2 * p + i][...], NN)
            grad_normed = part if grad_normed is None else grad_normed + part
    gain_grad_ref[...] += fold(grad_normed * scaled, jnp.sum)
    w = grad_normed * gain_ref[...]
    out_ref[...] = grad_hidden_ref[...] + root * (w - scaled * mean_rows(w * scaled))


def back(x, grad_hidden, gain, weights, grads):
    tokens, width = x.shape
    rows = pl.BlockSpec((TILE, width), lambda i: (i, 0))
    return pl.pallas_call(
        functools.partial(back_kernel, len(grads)),
        grid=(tokens // TILE,),
        in_specs=[
            rows,
            rows,
            pl.BlockSpec((1, width), lambda i: (0, 0)),
            *[pl.BlockSpec(w.shape, lambda i: (0, 0)) for w in weights],
            *[pl.BlockSpec((d.shape[0], TILE), lambda i: (0, i)) for d in grads],
        ],
        out_specs=[rows, pl.BlockSpec((8, width), lambda i: (0, 0))],
        out_shape=[
            jax.ShapeDtypeStruct((tokens, width), jnp.float32),
            jax.ShapeDtypeStruct((8, width), jnp.float32),
        ],
        cost_estimate=pl.CostEstimate(
            flops=6 * tokens * width * width, bytes_accessed=18 * tokens * width, transcendentals=0
        ),
        name="back",
    )(x, grad_hidden, gain, *weights, *grads)


GROUPS = ((0, 1, 2, 4), (3, 5, 6, 8), (7, 9, 10, 12), (11, 13, 14, 15))
FULL = 32
FAR = ((16, 0), (8, 3), (16, 0))


def exchange(x, bit, n):
    return lax.ppermute(x, AXIS, [(i, i ^ bit) for i in range(n)])


def tie(*values):
    return lax.optimization_barrier(values)


def next_group(group, step, n):
    bit, source = FAR[step]
    return [
        exchange(group[2:4], 2, n),
        exchange(group[3:4], 4, n),
        exchange(group[source : source + 1], bit, n),
    ]


def add(*terms):
    return functools.reduce(jnp.add, [t.astype(jnp.float32) for t in terms])


def send_group(terms, step, n):
    sums = [add(*t).astype(LOW) for t in terms]
    if step == 0:
        away = sums[1:]
        return [exchange(x, bit, n) for x, bit in zip(away, (2, 4, 8))], away
    away = [jnp.stack(sums[:2]), sums[2], sums[3]]
    return [exchange(x, bit, n) for x, bit in zip(away, (2, 4, FAR[step - 1][0]))], away


def arrivals(came, step):
    terms = [[], [], [came[0][0]], [came[0][1], came[1]]]
    terms[FAR[step - 1][1]].append(came[2])
    return terms


def sum_all(x, n):
    if n & (n - 1):
        return lax.psum(x, AXIS)
    bit = 1
    while bit < n:
        x = x + exchange(x, bit, n)
        bit *= 2
    return x


def gather_small(x, n):
    if n != FULL:
        return lax.all_gather(x, AXIS)
    x = jnp.stack([x, exchange(x, 1, n)])
    x = jnp.concatenate([x] + [exchange(x, bit, n) for bit in (2, 4, 6)])
    x = jnp.concatenate([x] + [exchange(x, bit, n) for bit in (8, 16, 24)])
    for axis, bit in ((0, 16), (1, 8), (2, 4), (3, 2), (4, 1)):
        x = x.reshape(2, 2, 2, 2, 2, -1)
        x = jnp.where((lax.axis_index(AXIS) // bit) % 2 == 1, jnp.flip(x, axis), x)
    return x.reshape(n, -1)


def on_device(n, *arguments):
    (
        inputs,
        block_ids,
        cotangent,
        first_gain,
        query_weight,
        key_weight,
        value_weight,
        output_weight,
        second_gain,
        up_weight,
        down_weight,
        query_scale,
    ) = arguments
    seqs, length, width = inputs.shape
    tokens = seqs * length
    depth = query_scale.shape[0]
    unit = depth // 2
    shard = first_gain.shape[0]
    me = lax.axis_index(AXIS)
    whole = n == FULL
    here = me if whole else jnp.zeros_like(me)
    core = (here % 2).reshape(1)
    slots = jnp.array([r for group in GROUPS for r in group], jnp.int32)
    place = jnp.bitwise_xor(here // 2, slots)

    early = jnp.stack([query_weight.T, key_weight.T, value_weight.T])
    late = jnp.stack([output_weight.T, up_weight.T, down_weight.T])
    gains = jnp.concatenate([first_gain, second_gain]).astype(jnp.float32)
    gains = gather_small(gains, n).reshape(n, 2, shard)
    gains = jnp.swapaxes(gains, 0, 1).reshape(2, width)

    ids = block_ids.reshape(1, tokens)
    row = lax.broadcasted_iota(jnp.int32, (EXTRA, tokens), 0)
    qx = ((ids == row) & (row < BLOCKS)).astype(LOW)
    kx = jnp.where(
        row < BLOCKS, jnp.where(ids > row, -1e30, 0.0), jnp.where(row < BLOCKS + 3, 1.0, 0.0)
    ).astype(LOW)
    last = block_ids[:, TILE - 1 :: TILE]
    seen = jnp.sum(block_ids[:, None, :] <= last[:, :, None], axis=-1)
    counts = ((seen + TILE - 1) // TILE).astype(jnp.int32)

    x = inputs.reshape(tokens, width)
    g = cotangent.reshape(tokens, width)
    factor = query_scale / math.sqrt(depth)
    mine_first = jnp.where(core[0] == 0, factor, jnp.roll(factor, unit))
    factor_rows = jnp.broadcast_to(mine_first[:, None], (depth, TILE))
    wide = x.astype(jnp.float32)
    root = lax.rsqrt(jnp.mean(wide * wide, axis=-1, keepdims=True) + EPSILON)
    normed = (wide * root * gains[0]).astype(LOW)

    def forward(mine, other, normed):
        return attention_forward(
            normed, mine.reshape(-1, width), other.reshape(-1, width), factor_rows * LOG2E,
            qx, kx, counts, depth, length,
        )

    mines, others, firsts = [], [], []
    if whole:
        mine = jnp.stack([early] + [exchange(early, bit, n) for bit in (2, 4, 8)])
        for step in range(4):
            other = exchange(mine, 1, n)
            mines.append(mine)
            others.append(other)
            if step < 3:
                came = next_group(mine, step, n)
                mine, normed = tie(mine, normed)
            result = forward(mine, other, normed)
            if step < 3:
                *came, first = tie(*came, result[0])
                result = [first, *result[1:]]
                mine = jnp.concatenate(came)
            firsts.append(result)
    else:
        both = lax.all_gather(early, AXIS, axis=1, tiled=True)
        both = both.reshape(3, -1, 2, unit, width)
        for group in GROUPS:
            rows = jnp.stack([both[:, r] for r in group])
            mines.append(rows[:, :, 0])
            others.append(rows[:, :, 1])
            firsts.append(forward(mines[-1], others[-1], normed))
    late = lax.all_gather(late, AXIS, axis=1, tiled=True)
    contexts = [context for _, context, _ in firsts]
    output, grad_hidden, *rest = middle(core, place, x, g, gains[1:], late, contexts, unit)
    grad_contexts, (keep, send, gain2_rows) = rest[:4], rest[4:]

    def backward(p, grad_context):
        qkv, context, lse = firsts[p]
        return attention_backward(
            qkv, context, grad_context, lse, qx, kx, counts, factor_rows, depth, length
        )

    def weight_grad(rows):
        return dot(rows, normed, NN).astype(LOW)

    grads, scale_parts = [None] * 4, []
    if whole:
        late_came = exchange(send, 1, n)
        came = None
        for p in (3, 2, 1, 0):
            grad_context = grad_contexts[p]
            if came is not None:
                *away, grad_context = tie(*away, grad_context)
            d, part = backward(p, grad_context)
            scale_parts.append(part)
            half = d.shape[0] // 2
            own_send = weight_grad(d[half:]).reshape(4, 3, unit, width)
            own_came = exchange(own_send, 1, n)
            own_keep = weight_grad(d[:half]).reshape(4, 3, unit, width)
            if p == 3:
                late_came, d = tie(late_came, d)
            else:
                *came, d = tie(*came, d)
            own_keep, own_came = tie(own_keep, own_came)
            grads[p] = d
            terms = [
                [
                    jnp.concatenate([own_keep[i], keep[4 * p + i]]),
                    jnp.concatenate([own_came[i], late_came[4 * p + i]]),
                ]
                for i in range(4)
            ]
            if came is not None:
                terms = [a + b for a, b in zip(terms, arrivals(came, p + 1))]
            came, away = send_group(terms, p, n)
        final = terms[0]
    else:
        for p in range(4):
            grads[p], part = backward(p, grad_contexts[p])
            scale_parts.append(part)
        order = jnp.argsort(slots)
        late_rows = jnp.stack([keep, send], axis=2)[order]
        own_rows = jnp.stack([weight_grad(d).reshape(2, 4, 3, unit, width) for d in grads])
        own_rows = own_rows.transpose(0, 2, 3, 1, 4, 5).reshape(16, 3, 2, unit, width)[order]
        rows = jnp.concatenate([own_rows, late_rows], axis=1).astype(jnp.float32)
        rows = rows.transpose(1, 0, 2, 3, 4).reshape(6, width, width)
        sums = lax.psum_scatter(rows, AXIS, scatter_dimension=1, tiled=True)

    weights = [w.reshape(-1, width) for pair in zip(mines, others) for w in pair]
    grad_inputs, gain1_rows = back(x, grad_hidden, gains[:1], weights, grads)
    if whole:
        *came, grad_inputs = tie(*came, grad_inputs)
        sums = add(*final, *came)
    scale_part = jnp.sum(functools.reduce(jnp.add, scale_parts), axis=1)
    scale_part = jnp.where(core[0] == 0, scale_part, jnp.roll(scale_part, unit))
    scale_part = scale_part / (factor * LOG2E) / math.sqrt(depth)
    grad_gain1, grad_gain2 = jnp.sum(gain1_rows, axis=0), jnp.sum(gain2_rows, axis=0)
    small = sum_all(jnp.concatenate([grad_gain1, grad_gain2, scale_part]), n)
    gain1 = lax.dynamic_slice_in_dim(small, me * shard, shard)
    gain2 = lax.dynamic_slice_in_dim(small, width + me * shard, shard)

    return (
        output.reshape(seqs, length, width),
        grad_inputs.reshape(seqs, length, width),
        gain1,
        sums[0].T,
        sums[1].T,
        sums[2].T,
        sums[3].T,
        gain2,
        sums[4].T,
        sums[5].T,
        small[2 * width :],
    )


def solution(mesh):
    rows, columns = P(AXIS), P(None, AXIS)
    in_specs = (rows, rows, rows, rows, *[columns] * 4, rows, columns, columns, P())
    out_specs = (rows, rows, rows, *[columns] * 4, rows, columns, columns, P())
    return jax.shard_map(
        functools.partial(on_device, mesh.shape[AXIS]),
        mesh=mesh,
        in_specs=in_specs,
        out_specs=out_specs,
        check_vma=False,
    )
```

```python
import functools
import math

import jax
import jax.numpy as jnp
from jax import lax
from jax.experimental import pallas as pl
from jax.experimental.pallas import tpu as pltpu
from jax.sharding import PartitionSpec as P

EPSILON = 1e-06
AXIS = "fsdp"
BLOCKS = 4
TILE = 256
EXTRA = 16
HEADS_PER_STEP = 4
LOW = jnp.bfloat16
LOG2E = math.log2(math.e)
LN2 = math.log(2.0)
NN = (((1,), (0,)), ((), ()))
NT = (((1,), (1,)), ((), ()))
TN = (((0,), (0,)), ((), ()))
TT = (((0,), (1,)), ((), ()))


def dot(left, right, dims):
    return lax.dot_general(left, right, dims, preferred_element_type=jnp.float32)


def three_rows(value, base, at):
    row = lax.broadcasted_iota(jnp.int32, (EXTRA, value.shape[1]), 0)
    first = value.astype(LOW).astype(jnp.float32)
    rest = value - first
    second = rest.astype(LOW).astype(jnp.float32)
    third = rest - second
    rows = jnp.where(row == at + 1, second, jnp.where(row == at + 2, third, base))
    return jnp.where(row == at, first, rows).astype(LOW)


def fold(x, op):
    return op(x.reshape(x.shape[0] // 8, 8, x.shape[1]), axis=0)


def for_each_tile(length, count_of, body):
    @pl.loop(0, length // TILE)
    def _(t):
        count = count_of(t)
        for n in range(1, length // TILE + 1):

            @pl.when(count == n)
            def _(n=n):
                body(pl.ds(pl.multiple_of(t * TILE, TILE), TILE), n)


def attention_forward_kernel(heads, depth, length, first, counts, *refs):
    if first:
        x_ref, gain_ref, *refs = refs
        *refs, normed_ref, kn, sb = refs
        x = x_ref[...].astype(jnp.float32)
        root = lax.rsqrt(jnp.mean(x * x, axis=-1, keepdims=True) + EPSILON)
        normed_ref[...] = (x * root * gain_ref[...]).astype(LOW)
    else:
        normed_ref, *refs, kn, sb = refs
    mine_ref, other_ref, factor_ref, qx_ref, kx_ref, qkv_ref, o_ref, lse_ref = refs
    s = pl.program_id(0)
    unit = depth // 2
    for at in range(0, length, TILE):
        normed = normed_ref[at : at + TILE, :]
        for part, w_ref in enumerate((mine_ref, other_ref)):
            y = dot(w_ref[...], normed, NT)
            for h in range(heads):
                for i in range(3):
                    rows = y[(3 * h + i) * unit : (3 * h + i + 1) * unit]
                    if i == 0:
                        rows = rows * factor_ref[part * unit : (part + 1) * unit, :]
                    start = h * depth + part * unit
                    qkv_ref[i, start : start + unit, at : at + TILE] = rows.astype(LOW)
    q_ref, k_ref, v_ref = qkv_ref.at[0], qkv_ref.at[1], qkv_ref.at[2]
    for h in range(heads):
        kn[h] = jnp.concatenate([k_ref[h * depth : (h + 1) * depth, :], kx_ref[...]], axis=0).T

    def tile(qs, n):
        qx = qx_ref[:, qs]
        peaks = [None] * (heads + 1)
        for h in range(heads + 1):
            out = total = None
            if h > 0:
                peak = jnp.max(peaks[h - 1], axis=0, keepdims=True)
            for c in range(n):
                ks = slice(c * TILE, (c + 1) * TILE)
                if h < heads:
                    q = jnp.concatenate([q_ref[h * depth : (h + 1) * depth, qs], qx], axis=0)
                    scores = dot(kn[h, ks, :], q, NN)
                    sb[h % 2, ks, :] = scores
                    part = fold(scores, jnp.max)
                    peaks[h] = part if c == 0 else jnp.maximum(peaks[h], part)
                if h > 0:
                    p = jnp.exp2(sb[(h - 1) % 2, ks, :] - peak)
                    part = fold(p, jnp.sum)
                    total = part if c == 0 else total + part
                    part = dot(v_ref[(h - 1) * depth : h * depth, ks], p.astype(LOW), NN)
                    out = part if c == 0 else out + part
            if h > 0:
                total = jnp.sum(total, axis=0, keepdims=True)
                o_ref[(h - 1) * depth : h * depth, qs] = (out * (1.0 / total)).astype(LOW)
                lse_ref[h - 1, :, qs] = peak + jnp.log2(total)

    for_each_tile(length, lambda t: counts[s, t], tile)


def attention_forward(source, gain, mine, other, factor, qx, kx, counts, depth, length):
    tokens, width = source.shape
    first = gain is not None
    seqs = tokens // length
    heads = mine.shape[0] * 2 // (3 * depth)
    group = heads * depth
    extra = pl.BlockSpec((EXTRA, length), lambda s, counts: (0, s))
    weight = pl.BlockSpec(mine.shape, lambda s, counts: (0, 0))
    sequence = pl.BlockSpec((length, width), lambda s, counts: (s, 0))
    gains = [pl.BlockSpec((1, width), lambda s, counts: (0, 0))] if first else []
    return pl.pallas_call(
        functools.partial(attention_forward_kernel, heads, depth, length, first),
        grid_spec=pltpu.PrefetchScalarGridSpec(
            num_scalar_prefetch=1,
            grid=(seqs,),
            in_specs=[
                sequence,
                *gains,
                weight,
                weight,
                pl.BlockSpec((depth, TILE), lambda s, counts: (0, 0)),
                extra,
                extra,
            ],
            out_specs=[
                pl.BlockSpec((3, group, length), lambda s, counts: (0, 0, s)),
                pl.BlockSpec((group, length), lambda s, counts: (0, s)),
                pl.BlockSpec((heads, 1, length), lambda s, counts: (0, 0, s)),
                *([sequence] if first else []),
            ],
            scratch_shapes=[
                pltpu.VMEM((heads, length, depth + EXTRA), LOW),
                pltpu.VMEM((2, length, TILE), jnp.float32),
            ],
        ),
        out_shape=[
            jax.ShapeDtypeStruct((3, group, tokens), LOW),
            jax.ShapeDtypeStruct((group, tokens), LOW),
            jax.ShapeDtypeStruct((heads, 1, tokens), jnp.float32),
            *([jax.ShapeDtypeStruct((tokens, width), LOW)] if first else []),
        ],
        cost_estimate=pl.CostEstimate(
            flops=4 * heads * 256 * length * tokens + 6 * group * tokens * width,
            bytes_accessed=2 * tokens * width + 8 * group * tokens,
            transcendentals=heads * length * tokens,
        ),
        name="attention_forward",
    )(counts, source, *([gain] if first else []), mine, other, factor, qx, kx)


def attention_backward_kernel(
    heads,
    depth,
    length,
    ahead,
    counts,
    q_ref,
    k_ref,
    v_ref,
    o_ref,
    do_ref,
    lse_ref,
    qx_ref,
    kx_ref,
    factor_ref,
    normed_ref,
    d_ref,
    scale_ref,
    keep_ref,
    send_ref,
    kn,
    vn,
    dka,
    dva,
    total,
):
    s = pl.program_id(0)
    unit = depth // 2

    @pl.when(s == 0)
    def _():
        scale_ref[...] = jnp.zeros_like(scale_ref)
        total[...] = jnp.zeros_like(total)

    dka[...] = jnp.zeros_like(dka)
    dva[...] = jnp.zeros_like(dva)
    ones = jnp.where(lax.broadcasted_iota(jnp.int32, (EXTRA, length), 0) < 3, 1.0, 0.0).astype(LOW)
    for h in range(heads):
        hs = slice(h * depth, (h + 1) * depth)
        kn[h] = jnp.concatenate([k_ref[hs, :], kx_ref[...]], axis=0).T
        vn[h] = jnp.concatenate([v_ref[hs, :], ones], axis=0).T

    def put(h, i, columns, value):
        for part in range(2):
            start = ((part * heads + h) * 3 + i) * unit
            rows = value[part * unit : (part + 1) * unit]
            d_ref[start : start + unit, columns] = rows.astype(LOW)

    def tile(qs, n):
        base = qx_ref[:, qs].astype(jnp.float32)
        queries, grads = [], []
        items = [(h, c) for h in range(heads) for c in range(n)]

        def first(i):
            h, c = items[i]
            hs, ks = slice(h * depth, (h + 1) * depth), slice(c * TILE, (c + 1) * TILE)
            if c == 0:
                q, do, o = q_ref[hs, qs], do_ref[hs, qs], o_ref[hs, qs]
                centre = jnp.sum(
                    do.astype(jnp.float32) * o.astype(jnp.float32), axis=0, keepdims=True
                )
                queries.append(
                    jnp.concatenate([q, three_rows(-lse_ref[h, :, qs], base, 4)], axis=0)
                )
                grads.append(jnp.concatenate([do, three_rows(-centre, 0.0, 0)], axis=0))
            return dot(kn[h, ks, :], queries[h], NN), dot(vn[h, ks, :], grads[h], NN)

        pending = [first(i) for i in range(min(ahead, len(items)))]
        dq = None
        for i, (h, c) in enumerate(items):
            if i + ahead < len(items):
                pending.append(first(i + ahead))
            scores, dp = pending[i]
            pending[i] = None
            hs, ks = slice(h * depth, (h + 1) * depth), slice(c * TILE, (c + 1) * TILE)
            p = jnp.exp2(scores)
            ds = (p * dp).astype(LOW)
            dva[hs, ks] += dot(do_ref[hs, qs], p.astype(LOW), NT)
            dka[hs, ks] += dot(q_ref[hs, qs], ds, NT)
            part = dot(k_ref[hs, ks], ds, NN)
            dq = part if c == 0 else dq + part
            if c == n - 1:
                put(h, 0, qs, dq * factor_ref[...])
                scale_ref[...] += dq * q_ref[hs, qs].astype(jnp.float32)

    for_each_tile(length, lambda t: counts[s, t], tile)
    for h in range(heads):
        put(h, 1, slice(None), dka[h * depth : (h + 1) * depth, :] * LN2)
        put(h, 2, slice(None), dva[h * depth : (h + 1) * depth, :])

    @pl.loop(0, normed_ref.shape[1] // TILE)
    def _(c):
        cs = pl.ds(pl.multiple_of(c * TILE, TILE), TILE)
        total[:, cs] += dot(d_ref[...], normed_ref[:, cs], NN)

    @pl.when(s == pl.num_programs(0) - 1)
    def _():
        half = total.shape[0] // 2
        keep_ref[...] = total[:half, :].astype(LOW)
        send_ref[...] = total[half:, :].astype(LOW)


def attention_backward(
    qkv, context, grad_context, lse, qx, kx, counts, factor, normed, depth, length
):
    _, group, tokens = qkv.shape
    width = normed.shape[1]
    heads, seqs = group // depth, tokens // length

    def third(i):
        return pl.BlockSpec((None, group, length), lambda s, counts: (i, 0, s))

    whole = pl.BlockSpec((group, length), lambda s, counts: (0, s))
    extra = pl.BlockSpec((EXTRA, length), lambda s, counts: (0, s))
    fixed = pl.BlockSpec((depth, TILE), lambda s, counts: (0, 0))
    return pl.pallas_call(
        functools.partial(attention_backward_kernel, heads, depth, length, 1),
        grid_spec=pltpu.PrefetchScalarGridSpec(
            num_scalar_prefetch=1,
            grid=(seqs,),
            in_specs=[
                third(0),
                third(1),
                third(2),
                whole,
                whole,
                pl.BlockSpec((heads, 1, length), lambda s, counts: (0, 0, s)),
                extra,
                extra,
                fixed,
                pl.BlockSpec((length, width), lambda s, counts: (s, 0)),
            ],
            out_specs=[
                pl.BlockSpec((3 * group, length), lambda s, counts: (0, s)),
                fixed,
                pl.BlockSpec((3 * group // 2, width), lambda s, counts: (0, 0)),
                pl.BlockSpec((3 * group // 2, width), lambda s, counts: (0, 0)),
            ],
            scratch_shapes=[
                pltpu.VMEM((heads, length, depth + EXTRA), LOW),
                pltpu.VMEM((heads, length, depth + EXTRA), LOW),
                pltpu.VMEM((group, length), jnp.float32),
                pltpu.VMEM((group, length), jnp.float32),
                pltpu.VMEM((3 * group, width), jnp.float32),
            ],
        ),
        out_shape=[
            jax.ShapeDtypeStruct((3 * group, tokens), LOW),
            jax.ShapeDtypeStruct((depth, TILE), jnp.float32),
            jax.ShapeDtypeStruct((3 * group // 2, width), LOW),
            jax.ShapeDtypeStruct((3 * group // 2, width), LOW),
        ],
        cost_estimate=pl.CostEstimate(
            flops=7 * heads * 256 * length * tokens + 6 * group * tokens * width,
            bytes_accessed=16 * group * tokens,
            transcendentals=heads * length * tokens,
        ),
        name="attention_backward",
    )(counts, qkv, qkv, qkv, context, grad_context, lse, qx, kx, factor, normed)


def mean_rows(x):
    return jnp.mean(x, axis=-1, keepdims=True)


def middle_kernel(
    unit,
    groups,
    core_ref,
    place_ref,
    x_ref,
    g_ref,
    gain_ref,
    w_ref,
    *rest,
):
    context_refs, rest = rest[:groups], rest[groups:]
    out_ref, grad_hidden_ref, *rest = rest
    grad_context_refs, rest = rest[:groups], rest[groups:]
    keep_ref, send_ref, gain_grad_ref, total, turned = rest
    step = pl.program_id(0)
    core = core_ref[0]
    heads = place_ref.shape[0] // groups

    def pieces():
        for j in range(groups * heads):
            for part in range(2):
                at = (2 * place_ref[j] + (core + part) % 2) * unit
                start = (2 * (j % heads) + part) * unit
                yield j // heads, slice(start, start + unit), pl.ds(pl.multiple_of(at, 8), unit)

    @pl.when(step == 0)
    def _():
        total[...] = jnp.zeros_like(total)
        gain_grad_ref[...] = jnp.zeros_like(gain_grad_ref)

    g = g_ref[...]
    gain = gain_ref[...]
    for p, rows, at in pieces():
        turned[at, :] = context_refs[p][rows, :].astype(jnp.float32)
    context = turned[...].astype(LOW).T
    hidden = x_ref[...].astype(jnp.float32) + dot(context, w_ref[0], NT)
    root = lax.rsqrt(mean_rows(hidden * hidden) + EPSILON)
    scaled = hidden * root
    normed = (scaled * gain).astype(LOW)
    upward = dot(normed, w_ref[1], NT)
    s = jax.nn.sigmoid(upward)
    activated = (upward * s).astype(LOW)
    out_ref[...] = (hidden + dot(activated, w_ref[2], NT)).astype(LOW)
    slope = s * (1.0 + upward * (1.0 - s))
    grad_upward = (dot(g, w_ref[2], NN) * slope).astype(LOW)
    total[2] += dot(g.T, activated, NN)
    grad_normed = dot(grad_upward, w_ref[1], NN)
    total[1] += dot(grad_upward.T, normed, NN)
    gain_grad_ref[...] += fold(grad_normed * scaled, jnp.sum)
    w = grad_normed * gain
    grad_hidden = g.astype(jnp.float32) + root * (w - scaled * mean_rows(w * scaled))
    grad_hidden_ref[...] = grad_hidden
    branch = grad_hidden.astype(LOW)
    turned[...] = dot(branch, w_ref[0], NN).astype(LOW).T.astype(jnp.float32)
    for p, rows, at in pieces():
        grad_context_refs[p][rows, :] = turned[at, :].astype(LOW)
    total[0] += dot(branch.T, context, NN)

    @pl.when(step == pl.num_programs(0) - 1)
    def _():
        @pl.loop(0, groups * heads)
        def _(j):
            for i in range(3):
                at = pl.multiple_of((2 * place_ref[j] + core) * unit, 8)
                keep_ref[j, i] = total[i, pl.ds(at, unit), :].astype(LOW)
                at = pl.multiple_of((2 * place_ref[j] + 1 - core) * unit, 8)
                send_ref[j, i] = total[i, pl.ds(at, unit), :].astype(LOW)


def middle(core, place, x, g, gain, weight, contexts, unit):
    tokens, width = x.shape
    chips = width // (2 * unit)
    rows = pl.BlockSpec((TILE, width), lambda i, core, place: (i, 0))
    columns = [
        pl.BlockSpec((c.shape[0], TILE), lambda i, core, place: (0, i)) for c in contexts
    ]
    once = pl.Buffered(1)
    half = pl.BlockSpec(
        (chips, 3, unit, width), lambda i, core, place: (0, 0, 0, 0), pipeline_mode=once
    )
    halves = jax.ShapeDtypeStruct((chips, 3, unit, width), LOW)
    return pl.pallas_call(
        functools.partial(middle_kernel, unit, len(contexts)),
        grid_spec=pltpu.PrefetchScalarGridSpec(
            num_scalar_prefetch=2,
            grid=(tokens // TILE,),
            in_specs=[
                rows,
                rows,
                pl.BlockSpec((1, width), lambda i, core, place: (0, 0)),
                pl.BlockSpec(
                    (3, width, width), lambda i, core, place: (0, 0, 0), pipeline_mode=once
                ),
                *columns,
            ],
            out_specs=[
                rows,
                rows,
                *columns,
                half,
                half,
                pl.BlockSpec((8, width), lambda i, core, place: (0, 0)),
            ],
            scratch_shapes=[
                pltpu.VMEM((3, width, width), jnp.float32),
                pltpu.VMEM((width, TILE), jnp.float32),
            ],
        ),
        out_shape=[
            jax.ShapeDtypeStruct((tokens, width), LOW),
            jax.ShapeDtypeStruct((tokens, width), jnp.float32),
            *[jax.ShapeDtypeStruct(c.shape, LOW) for c in contexts],
            halves,
            halves,
            jax.ShapeDtypeStruct((8, width), jnp.float32),
        ],
        compiler_params=pltpu.CompilerParams(vmem_limit_bytes=66_000_000),
        cost_estimate=pl.CostEstimate(
            flops=18 * tokens * width * width,
            bytes_accessed=14 * tokens * width + 12 * width * width,
            transcendentals=tokens * width,
        ),
        name="middle",
    )(core, place, x, g, gain, weight, *contexts)


def back_kernel(groups, x_ref, grad_hidden_ref, gain_ref, *rest):
    w_refs, d_refs, (out_ref, gain_grad_ref) = rest[: 2 * groups], rest[2 * groups : -2], rest[-2:]

    @pl.when(pl.program_id(0) == 0)
    def _():
        gain_grad_ref[...] = jnp.zeros_like(gain_grad_ref)

    x = x_ref[...].astype(jnp.float32)
    root = lax.rsqrt(mean_rows(x * x) + EPSILON)
    scaled = x * root
    grad_normed = None
    for p in range(groups):
        d = d_refs[p][...].T
        rows = d.shape[1] // 2
        for i in range(2):
            part = dot(d[:, i * rows : (i + 1) * rows], w_refs[2 * p + i][...], NN)
            grad_normed = part if grad_normed is None else grad_normed + part
    gain_grad_ref[...] += fold(grad_normed * scaled, jnp.sum)
    w = grad_normed * gain_ref[...]
    out_ref[...] = grad_hidden_ref[...] + root * (w - scaled * mean_rows(w * scaled))


def back(x, grad_hidden, gain, weights, grads):
    tokens, width = x.shape
    rows = pl.BlockSpec((TILE, width), lambda i: (i, 0))
    return pl.pallas_call(
        functools.partial(back_kernel, len(grads)),
        grid=(tokens // TILE,),
        in_specs=[
            rows,
            rows,
            pl.BlockSpec((1, width), lambda i: (0, 0)),
            *[pl.BlockSpec(w.shape, lambda i: (0, 0)) for w in weights],
            *[pl.BlockSpec((d.shape[0], TILE), lambda i: (0, i)) for d in grads],
        ],
        out_specs=[rows, pl.BlockSpec((8, width), lambda i: (0, 0))],
        out_shape=[
            jax.ShapeDtypeStruct((tokens, width), jnp.float32),
            jax.ShapeDtypeStruct((8, width), jnp.float32),
        ],
        cost_estimate=pl.CostEstimate(
            flops=6 * tokens * width * width, bytes_accessed=18 * tokens * width, transcendentals=0
        ),
        name="back",
    )(x, grad_hidden, gain, *weights, *grads)


def combine_kernel(x_at, z_at, y_at, last, own_ref, own_came_ref, late_ref, late_came_ref, *refs):
    if x_at is not None:
        came_x, came_y, came_z, *refs = refs
    for kind, (keep, came) in enumerate(((own_ref, own_came_ref), (late_ref, late_came_ref))):
        sums = [keep[i, 0].astype(jnp.float32) + came[i, 0].astype(jnp.float32) for i in range(4)]
        if x_at is not None:
            for i in range(2):
                sums[x_at + i] += came_x[i, kind, 0].astype(jnp.float32)
            sums[y_at] += came_y[kind, 0].astype(jnp.float32)
            sums[z_at] += came_z[kind, 0].astype(jnp.float32)
        if last:
            own, *sums = sums
            refs[0][kind, 0] = own
            for ref, value in zip(refs[1:], sums):
                ref[kind, 0] = value.astype(LOW)
        else:
            refs[0][0, kind, 0] = sums[0].astype(LOW)
            refs[0][1, kind, 0] = sums[1].astype(LOW)
            refs[1][kind, 0] = sums[2].astype(LOW)
            refs[2][kind, 0] = sums[3].astype(LOW)


def combine(group, own, own_came, late, late_came, came):
    _, three, unit, width = own.shape
    last = group == 0

    def block(*lead, at=0):
        return pl.BlockSpec((*lead, 1, unit, width), lambda i: (at, *[0] * (len(lead) - 1), i, 0, 0))

    one = jax.ShapeDtypeStruct((2, three, unit, width), LOW)
    two = jax.ShapeDtypeStruct((2, 2, three, unit, width), LOW)
    full = jax.ShapeDtypeStruct((2, three, unit, width), jnp.float32)
    places = (None, None, None)
    if came is not None:
        places = (2, FAR[group][1], 3)
    return pl.pallas_call(
        functools.partial(combine_kernel, *places, last),
        grid=(three,),
        in_specs=[block(4), block(4), block(4, at=group), block(4, at=group)]
        + ([] if came is None else [block(2, 2), block(2), block(2)]),
        out_specs=[block(2)] * 4 if last else [block(2, 2), block(2), block(2)],
        out_shape=[full, one, one, one] if last else [two, one, one],
        cost_estimate=pl.CostEstimate(
            flops=0, bytes_accessed=40 * three * unit * width, transcendentals=0
        ),
        name="combine",
    )(own, own_came, late, late_came, *(came or []))


GROUPS = ((0, 1, 2, 4), (3, 5, 6, 8), (7, 9, 10, 12), (11, 13, 14, 15))
FULL = 32
FAR = ((16, 0), (8, 3), (16, 0))


def exchange(x, bit, n):
    return lax.ppermute(x, AXIS, [(i, i ^ bit) for i in range(n)])


def tie(*values):
    return lax.optimization_barrier(values)


def next_group(group, step, n):
    bit, source = FAR[step]
    return [
        exchange(group[2:4], 2, n),
        exchange(group[3:4], 4, n),
        exchange(group[source : source + 1], bit, n),
    ]


def add(*terms):
    return functools.reduce(jnp.add, [t.astype(jnp.float32) for t in terms])


def sum_all(x, n):
    if n != FULL:
        return lax.psum(x, AXIS)
    x = x + exchange(x, 1, n)
    for bits in ((2, 4, 6), (8, 16, 24)):
        first, second, third = [exchange(x, bit, n) for bit in bits]
        x = (x + first) + (second + third)
    return x


def on_device(n, *arguments):
    (
        inputs,
        block_ids,
        cotangent,
        first_gain,
        query_weight,
        key_weight,
        value_weight,
        output_weight,
        second_gain,
        up_weight,
        down_weight,
        query_scale,
    ) = arguments
    seqs, length, width = inputs.shape
    tokens = seqs * length
    depth = query_scale.shape[0]
    unit = depth // 2
    shard = first_gain.shape[0]
    me = lax.axis_index(AXIS)
    whole = n == FULL
    here = me if whole else jnp.zeros_like(me)
    core = (here % 2).reshape(1)
    slots = jnp.array([r for group in GROUPS for r in group], jnp.int32)
    place = jnp.bitwise_xor(here // 2, slots)

    early = jnp.stack([query_weight.T, key_weight.T, value_weight.T])
    late = jnp.stack([output_weight.T, up_weight.T, down_weight.T])
    gains = jnp.concatenate([first_gain, second_gain]).astype(jnp.float32)
    if whole:
        relative = jnp.stack([gains, exchange(gains, 1, n)])
        relative = jnp.concatenate([relative] + [exchange(relative, b, n) for b in (2, 4, 6)])
        relative, early = tie(relative, early)
        relative = jnp.concatenate([relative] + [exchange(relative, b, n) for b in (8, 16, 24)])
        index = jnp.arange(n)
        chosen = index[:, None] == jnp.bitwise_xor(index, me)[None, :]
        gains = dot(chosen.astype(LOW), relative.astype(LOW), NN)
    else:
        gains = lax.all_gather(gains, AXIS)
    gains = jnp.swapaxes(gains.reshape(n, 2, shard), 0, 1).reshape(2, width)

    ids = block_ids.reshape(1, tokens)
    row = lax.broadcasted_iota(jnp.int32, (EXTRA, tokens), 0)
    qx = ((ids == row) & (row < BLOCKS)).astype(LOW)
    kx = jnp.where(
        row < BLOCKS, jnp.where(ids > row, -1e30, 0.0), jnp.where(row < BLOCKS + 3, 1.0, 0.0)
    ).astype(LOW)
    last = block_ids[:, TILE - 1 :: TILE]
    seen = jnp.sum(block_ids[:, None, :] <= last[:, :, None], axis=-1)
    counts = ((seen + TILE - 1) // TILE).astype(jnp.int32)

    x = inputs.reshape(tokens, width)
    g = cotangent.reshape(tokens, width)
    factor = query_scale / math.sqrt(depth)
    mine_first = jnp.where(core[0] == 0, factor, jnp.roll(factor, unit))
    factor_rows = jnp.broadcast_to(mine_first[:, None], (depth, TILE))

    def forward(mine, other, source, gain=None):
        return attention_forward(
            source, gain, mine.reshape(-1, width), other.reshape(-1, width), factor_rows * LOG2E,
            qx, kx, counts, depth, length,
        )

    mines, others, firsts = [], [], []
    if whole:
        mine = jnp.stack([early] + [exchange(early, bit, n) for bit in (2, 4, 8)])
        mine, late, gains = tie(mine, late, gains)
        late = lax.all_gather(late, AXIS, axis=1, tiled=True)
        source, gain = x, gains[:1]
        for step in range(4):
            other = exchange(mine, 1, n)
            mines.append(mine)
            others.append(other)
            if step < 3:
                came = next_group(mine, step, n)
            result = forward(mine, other, source, gain)
            if step == 0:
                *result, normed = result
                source, gain = normed, None
            if step < 3:
                *came, first = tie(*came, result[0])
                result = [first, *result[1:]]
                mine = jnp.concatenate(came)
            firsts.append(result)
    else:
        both = lax.all_gather(early, AXIS, axis=1, tiled=True)
        both = both.reshape(3, -1, 2, unit, width)
        source, gain = x, gains[:1]
        for group in GROUPS:
            rows = jnp.stack([both[:, r] for r in group])
            mines.append(rows[:, :, 0])
            others.append(rows[:, :, 1])
            result = forward(mines[-1], others[-1], source, gain)
            if gain is not None:
                *result, normed = result
                source, gain = normed, None
            firsts.append(result)
        late = lax.all_gather(late, AXIS, axis=1, tiled=True)
    contexts = [context for _, context, _ in firsts]
    output, grad_hidden, *rest = middle(core, place, x, g, gains[1:], late, contexts, unit)
    grad_contexts, (keep, send, gain2_rows) = rest[:4], rest[4:]

    def backward(p, grad_context):
        qkv, context, lse = firsts[p]
        return attention_backward(
            qkv, context, grad_context, lse, qx, kx, counts, factor_rows, normed, depth, length
        )

    grads, scale_parts = [None] * 4, []
    if whole:
        late_came = exchange(send, 1, n)
        came = away = None
        for p in (3, 2, 1, 0):
            grad_context = grad_contexts[p]
            if away is not None:
                *away, grad_context = tie(*away, grad_context)
            d, part, own_keep, own_send = backward(p, grad_context)
            scale_parts.append(part)
            if p == 3:
                late_came, own_send = tie(late_came, own_send)
            else:
                *came, own_send = tie(*came, own_send)
            grads[p] = d
            own_came = exchange(own_send.reshape(4, 3, unit, width), 1, n)
            own_keep = own_keep.reshape(4, 3, unit, width)
            away = combine(p, own_keep, own_came, keep, late_came, came)
            if p == 0:
                final, *away = away
            far = 8 if p == 0 else FAR[p - 1][0]
            came = [exchange(a, bit, n) for a, bit in zip(away, (2, 4, far))]
    else:
        own_rows = []
        for p in range(4):
            grads[p], part, *rows = backward(p, grad_contexts[p])
            scale_parts.append(part)
            own_rows.append(jnp.stack(rows).reshape(2, 4, 3, unit, width))
        order = jnp.argsort(slots)
        late_rows = jnp.stack([keep, send], axis=2)[order]
        own_rows = jnp.stack(own_rows).transpose(0, 2, 3, 1, 4, 5)
        own_rows = own_rows.reshape(16, 3, 2, unit, width)[order]
        rows = jnp.concatenate([own_rows, late_rows], axis=1).astype(jnp.float32)
        rows = rows.transpose(1, 0, 2, 3, 4).reshape(6, width, width)
        sums = lax.psum_scatter(rows, AXIS, scatter_dimension=1, tiled=True)

    weights = [w.reshape(-1, width) for pair in zip(mines, others) for w in pair]
    if whole:
        *away, d = tie(*away, grads[0])
        grads[0] = d
    grad_inputs, gain1_rows = back(x, grad_hidden, gains[:1], weights, grads)
    if whole:
        *came, gain1_rows = tie(*came, gain1_rows)
        sums = add(final, *came).reshape(6, unit, width)
    scale_part = jnp.sum(functools.reduce(jnp.add, scale_parts), axis=1)
    scale_part = jnp.where(core[0] == 0, scale_part, jnp.roll(scale_part, unit))
    scale_part = scale_part / (factor * LOG2E) / math.sqrt(depth)
    grad_gain1, grad_gain2 = jnp.sum(gain1_rows, axis=0), jnp.sum(gain2_rows, axis=0)
    small = sum_all(jnp.concatenate([grad_gain1, grad_gain2, scale_part]), n)
    gain1 = lax.dynamic_slice_in_dim(small, me * shard, shard)
    gain2 = lax.dynamic_slice_in_dim(small, width + me * shard, shard)

    return (
        output.reshape(seqs, length, width),
        grad_inputs.reshape(seqs, length, width),
        gain1,
        sums[0].T,
        sums[1].T,
        sums[2].T,
        sums[3].T,
        gain2,
        sums[4].T,
        sums[5].T,
        small[2 * width :],
    )


def solution(mesh):
    rows, columns = P(AXIS), P(None, AXIS)
    in_specs = (rows, rows, rows, rows, *[columns] * 4, rows, columns, columns, P())
    out_specs = (rows, rows, rows, *[columns] * 4, rows, columns, columns, P())
    return jax.shard_map(
        functools.partial(on_device, mesh.shape[AXIS]),
        mesh=mesh,
        in_specs=in_specs,
        out_specs=out_specs,
        check_vma=False,
    )
```

```python
import functools
import math

import jax
import jax.numpy as jnp
from jax import lax
from jax.experimental import pallas as pl
from jax.experimental.pallas import tpu as pltpu
from jax.sharding import PartitionSpec as P

EPSILON = 1e-06
AXIS = "fsdp"
BLOCKS = 4
TILE = 256
EXTRA = 16
HEADS_PER_STEP = 4
LOW = jnp.bfloat16
LOG2E = math.log2(math.e)
LN2 = math.log(2.0)
NN = (((1,), (0,)), ((), ()))
NT = (((1,), (1,)), ((), ()))
TN = (((0,), (0,)), ((), ()))
TT = (((0,), (1,)), ((), ()))


def dot(left, right, dims):
    return lax.dot_general(left, right, dims, preferred_element_type=jnp.float32)


def three_rows(value, base, at):
    row = lax.broadcasted_iota(jnp.int32, (EXTRA, value.shape[1]), 0)
    first = value.astype(LOW).astype(jnp.float32)
    rest = value - first
    second = rest.astype(LOW).astype(jnp.float32)
    third = rest - second
    rows = jnp.where(row == at + 1, second, jnp.where(row == at + 2, third, base))
    return jnp.where(row == at, first, rows).astype(LOW)


def fold(x, op):
    return op(x.reshape(x.shape[0] // 8, 8, x.shape[1]), axis=0)


def for_each_tile(length, count_of, body):
    @pl.loop(0, length // TILE)
    def _(t):
        count = count_of(t)
        for n in range(1, length // TILE + 1):

            @pl.when(count == n)
            def _(n=n):
                body(pl.ds(pl.multiple_of(t * TILE, TILE), TILE), n)


def attention_forward_kernel(heads, depth, length, first, counts, *refs):
    if first:
        x_ref, gain_ref, *refs = refs
        *refs, normed_ref, kn, sb, weight = refs
        x = x_ref[...].astype(jnp.float32)
        root = lax.rsqrt(jnp.mean(x * x, axis=-1, keepdims=True) + EPSILON)
        normed_ref[...] = (x * root * gain_ref[...]).astype(LOW)
    else:
        normed_ref, *refs, kn, sb, weight = refs
    mine_ref, other_ref, factor_ref, qx_ref, kx_ref, qkv_ref, o_ref, lse_ref = refs
    s = pl.program_id(0)
    unit = depth // 2
    half = mine_ref.shape[0]

    @pl.when(s == 0)
    def _():
        weight[:half, :] = mine_ref[...]
        weight[half:, :] = other_ref[...]

    for at in range(0, length, TILE):
        y = dot(weight[...], normed_ref[at : at + TILE, :], NT)
        for part in range(2):
            for h in range(heads):
                for i in range(3):
                    start = part * half + (3 * h + i) * unit
                    rows = y[start : start + unit]
                    if i == 0:
                        rows = rows * factor_ref[part * unit : (part + 1) * unit, :]
                    start = h * depth + part * unit
                    qkv_ref[i, start : start + unit, at : at + TILE] = rows.astype(LOW)
    q_ref, k_ref, v_ref = qkv_ref.at[0], qkv_ref.at[1], qkv_ref.at[2]
    for h in range(heads):
        kn[h] = jnp.concatenate([k_ref[h * depth : (h + 1) * depth, :], kx_ref[...]], axis=0).T

    def tile(qs, n):
        qx = qx_ref[:, qs]
        peaks = [None] * (heads + 1)
        for h in range(heads + 1):
            out = total = None
            if h > 0:
                peak = jnp.max(peaks[h - 1], axis=0, keepdims=True)
            for c in range(n):
                ks = slice(c * TILE, (c + 1) * TILE)
                if h < heads:
                    q = jnp.concatenate([q_ref[h * depth : (h + 1) * depth, qs], qx], axis=0)
                    scores = dot(kn[h, ks, :], q, NN)
                    sb[h % 2, ks, :] = scores
                    part = fold(scores, jnp.max)
                    peaks[h] = part if c == 0 else jnp.maximum(peaks[h], part)
                if h > 0:
                    p = jnp.exp2(sb[(h - 1) % 2, ks, :] - peak)
                    part = fold(p, jnp.sum)
                    total = part if c == 0 else total + part
                    part = dot(v_ref[(h - 1) * depth : h * depth, ks], p.astype(LOW), NN)
                    out = part if c == 0 else out + part
            if h > 0:
                total = jnp.sum(total, axis=0, keepdims=True)
                o_ref[(h - 1) * depth : h * depth, qs] = (out * (1.0 / total)).astype(LOW)
                lse_ref[h - 1, :, qs] = peak + jnp.log2(total)

    for_each_tile(length, lambda t: counts[s, t], tile)


def attention_forward(source, gain, mine, other, factor, qx, kx, counts, depth, length):
    tokens, width = source.shape
    first = gain is not None
    seqs = tokens // length
    heads = mine.shape[0] * 2 // (3 * depth)
    group = heads * depth
    extra = pl.BlockSpec((EXTRA, length), lambda s, counts: (0, s))
    weight = pl.BlockSpec(mine.shape, lambda s, counts: (0, 0))
    sequence = pl.BlockSpec((length, width), lambda s, counts: (s, 0))
    gains = [pl.BlockSpec((1, width), lambda s, counts: (0, 0))] if first else []
    return pl.pallas_call(
        functools.partial(attention_forward_kernel, heads, depth, length, first),
        grid_spec=pltpu.PrefetchScalarGridSpec(
            num_scalar_prefetch=1,
            grid=(seqs,),
            in_specs=[
                sequence,
                *gains,
                weight,
                weight,
                pl.BlockSpec((depth, TILE), lambda s, counts: (0, 0)),
                extra,
                extra,
            ],
            out_specs=[
                pl.BlockSpec((3, group, length), lambda s, counts: (0, 0, s)),
                pl.BlockSpec((group, length), lambda s, counts: (0, s)),
                pl.BlockSpec((heads, 1, length), lambda s, counts: (0, 0, s)),
                *([sequence] if first else []),
            ],
            scratch_shapes=[
                pltpu.VMEM((heads, length, depth + EXTRA), LOW),
                pltpu.VMEM((2, length, TILE), jnp.float32),
                pltpu.VMEM((3 * group, width), LOW),
            ],
        ),
        out_shape=[
            jax.ShapeDtypeStruct((3, group, tokens), LOW),
            jax.ShapeDtypeStruct((group, tokens), LOW),
            jax.ShapeDtypeStruct((heads, 1, tokens), jnp.float32),
            *([jax.ShapeDtypeStruct((tokens, width), LOW)] if first else []),
        ],
        cost_estimate=pl.CostEstimate(
            flops=4 * heads * 256 * length * tokens + 6 * group * tokens * width,
            bytes_accessed=2 * tokens * width + 8 * group * tokens,
            transcendentals=heads * length * tokens,
        ),
        name="attention_forward",
    )(counts, source, *([gain] if first else []), mine, other, factor, qx, kx)


def attention_backward_kernel(
    heads,
    depth,
    length,
    ahead,
    counts,
    q_ref,
    k_ref,
    v_ref,
    o_ref,
    do_ref,
    lse_ref,
    qx_ref,
    kx_ref,
    factor_ref,
    normed_ref,
    mine_ref,
    other_ref,
    d_ref,
    scale_ref,
    keep_ref,
    send_ref,
    gain_ref,
    kn,
    vn,
    dka,
    dva,
    total,
):
    s = pl.program_id(0)
    unit = depth // 2

    @pl.when(s == 0)
    def _():
        scale_ref[...] = jnp.zeros_like(scale_ref)
        total[...] = jnp.zeros_like(total)

    dka[...] = jnp.zeros_like(dka)
    dva[...] = jnp.zeros_like(dva)
    ones = jnp.where(lax.broadcasted_iota(jnp.int32, (EXTRA, length), 0) < 3, 1.0, 0.0).astype(LOW)
    for h in range(heads):
        hs = slice(h * depth, (h + 1) * depth)
        kn[h] = jnp.concatenate([k_ref[hs, :], kx_ref[...]], axis=0).T
        vn[h] = jnp.concatenate([v_ref[hs, :], ones], axis=0).T

    def put(h, i, columns, value):
        for part in range(2):
            start = ((part * heads + h) * 3 + i) * unit
            rows = value[part * unit : (part + 1) * unit]
            d_ref[start : start + unit, columns] = rows.astype(LOW)

    def tile(qs, n):
        base = qx_ref[:, qs].astype(jnp.float32)
        queries, grads = [], []
        items = [(h, c) for h in range(heads) for c in range(n)]

        def first(i):
            h, c = items[i]
            hs, ks = slice(h * depth, (h + 1) * depth), slice(c * TILE, (c + 1) * TILE)
            if c == 0:
                q, do, o = q_ref[hs, qs], do_ref[hs, qs], o_ref[hs, qs]
                centre = jnp.sum(
                    do.astype(jnp.float32) * o.astype(jnp.float32), axis=0, keepdims=True
                )
                queries.append(
                    jnp.concatenate([q, three_rows(-lse_ref[h, :, qs], base, 4)], axis=0)
                )
                grads.append(jnp.concatenate([do, three_rows(-centre, 0.0, 0)], axis=0))
            return dot(kn[h, ks, :], queries[h], NN), dot(vn[h, ks, :], grads[h], NN)

        pending = [first(i) for i in range(min(ahead, len(items)))]
        dq = None
        for i, (h, c) in enumerate(items):
            if i + ahead < len(items):
                pending.append(first(i + ahead))
            scores, dp = pending[i]
            pending[i] = None
            hs, ks = slice(h * depth, (h + 1) * depth), slice(c * TILE, (c + 1) * TILE)
            p = jnp.exp2(scores)
            ds = (p * dp).astype(LOW)
            dva[hs, ks] += dot(do_ref[hs, qs], p.astype(LOW), NT)
            dka[hs, ks] += dot(q_ref[hs, qs], ds, NT)
            part = dot(k_ref[hs, ks], ds, NN)
            dq = part if c == 0 else dq + part
            if c == n - 1:
                put(h, 0, qs, dq * factor_ref[...])
                scale_ref[...] += dq * q_ref[hs, qs].astype(jnp.float32)

    for_each_tile(length, lambda t: counts[s, t], tile)
    for h in range(heads):
        put(h, 1, slice(None), dka[h * depth : (h + 1) * depth, :] * LN2)
        put(h, 2, slice(None), dva[h * depth : (h + 1) * depth, :])

    @pl.loop(0, normed_ref.shape[1] // TILE)
    def _(c):
        cs = pl.ds(pl.multiple_of(c * TILE, TILE), TILE)
        total[:, cs] += dot(d_ref[...], normed_ref[:, cs], NN)

    @pl.when(s == pl.num_programs(0) - 1)
    def _():
        half = total.shape[0] // 2
        keep_ref[...] = total[:half, :].astype(LOW)
        send_ref[...] = total[half:, :].astype(LOW)
        mine = total[:half, :] * mine_ref[...].astype(jnp.float32)
        other = total[half:, :] * other_ref[...].astype(jnp.float32)
        gain_ref[...] = fold(mine, jnp.sum) + fold(other, jnp.sum)


def attention_backward(
    qkv, context, grad_context, lse, qx, kx, counts, factor, normed, mine, other, depth, length
):
    _, group, tokens = qkv.shape
    width = normed.shape[1]
    heads, seqs = group // depth, tokens // length

    def third(i):
        return pl.BlockSpec((None, group, length), lambda s, counts: (i, 0, s))

    whole = pl.BlockSpec((group, length), lambda s, counts: (0, s))
    extra = pl.BlockSpec((EXTRA, length), lambda s, counts: (0, s))
    fixed = pl.BlockSpec((depth, TILE), lambda s, counts: (0, 0))
    half = pl.BlockSpec((3 * group // 2, width), lambda s, counts: (0, 0))
    return pl.pallas_call(
        functools.partial(attention_backward_kernel, heads, depth, length, 2),
        grid_spec=pltpu.PrefetchScalarGridSpec(
            num_scalar_prefetch=1,
            grid=(seqs,),
            in_specs=[
                third(0),
                third(1),
                third(2),
                whole,
                whole,
                pl.BlockSpec((heads, 1, length), lambda s, counts: (0, 0, s)),
                extra,
                extra,
                fixed,
                pl.BlockSpec((length, width), lambda s, counts: (s, 0)),
                half,
                half,
            ],
            out_specs=[
                pl.BlockSpec((3 * group, length), lambda s, counts: (0, s)),
                fixed,
                half,
                half,
                pl.BlockSpec((8, width), lambda s, counts: (0, 0)),
            ],
            scratch_shapes=[
                pltpu.VMEM((heads, length, depth + EXTRA), LOW),
                pltpu.VMEM((heads, length, depth + EXTRA), LOW),
                pltpu.VMEM((group, length), jnp.float32),
                pltpu.VMEM((group, length), jnp.float32),
                pltpu.VMEM((3 * group, width), jnp.float32),
            ],
        ),
        out_shape=[
            jax.ShapeDtypeStruct((3 * group, tokens), LOW),
            jax.ShapeDtypeStruct((depth, TILE), jnp.float32),
            jax.ShapeDtypeStruct((3 * group // 2, width), LOW),
            jax.ShapeDtypeStruct((3 * group // 2, width), LOW),
            jax.ShapeDtypeStruct((8, width), jnp.float32),
        ],
        cost_estimate=pl.CostEstimate(
            flops=7 * heads * 256 * length * tokens + 6 * group * tokens * width,
            bytes_accessed=16 * group * tokens,
            transcendentals=heads * length * tokens,
        ),
        name="attention_backward",
    )(counts, qkv, qkv, qkv, context, grad_context, lse, qx, kx, factor, normed, mine, other)


def mean_rows(x):
    return jnp.mean(x, axis=-1, keepdims=True)


def middle_kernel(
    unit,
    groups,
    core_ref,
    place_ref,
    x_ref,
    g_ref,
    gain_ref,
    w_ref,
    *rest,
):
    context_refs, rest = rest[:groups], rest[groups:]
    out_ref, grad_hidden_ref, *rest = rest
    grad_context_refs, rest = rest[:groups], rest[groups:]
    keep_ref, send_ref, gain_grad_ref, total, turned = rest
    step = pl.program_id(0)
    core = core_ref[0]
    heads = place_ref.shape[0] // groups

    def pieces():
        for j in range(groups * heads):
            for part in range(2):
                at = (2 * place_ref[j] + (core + part) % 2) * unit
                start = (2 * (j % heads) + part) * unit
                yield j // heads, slice(start, start + unit), pl.ds(pl.multiple_of(at, 8), unit)

    @pl.when(step == 0)
    def _():
        total[...] = jnp.zeros_like(total)
        gain_grad_ref[...] = jnp.zeros_like(gain_grad_ref)

    g = g_ref[...]
    gain = gain_ref[...]
    for p, rows, at in pieces():
        turned[at, :] = context_refs[p][rows, :].astype(jnp.float32)
    context = turned[...].astype(LOW).T
    hidden = x_ref[...].astype(jnp.float32) + dot(context, w_ref[0], NT)
    root = lax.rsqrt(mean_rows(hidden * hidden) + EPSILON)
    scaled = hidden * root
    normed = (scaled * gain).astype(LOW)
    upward = dot(normed, w_ref[1], NT)
    s = jax.nn.sigmoid(upward)
    activated = (upward * s).astype(LOW)
    out_ref[...] = (hidden + dot(activated, w_ref[2], NT)).astype(LOW)
    slope = s * (1.0 + upward * (1.0 - s))
    grad_upward = (dot(g, w_ref[2], NN) * slope).astype(LOW)
    total[2] += dot(g.T, activated, NN)
    grad_normed = dot(grad_upward, w_ref[1], NN)
    total[1] += dot(grad_upward.T, normed, NN)
    gain_grad_ref[...] += fold(grad_normed * scaled, jnp.sum)
    w = grad_normed * gain
    grad_hidden = g.astype(jnp.float32) + root * (w - scaled * mean_rows(w * scaled))
    grad_hidden_ref[...] = grad_hidden
    branch = grad_hidden.astype(LOW)
    turned[...] = dot(branch, w_ref[0], NN).astype(LOW).T.astype(jnp.float32)
    for p, rows, at in pieces():
        grad_context_refs[p][rows, :] = turned[at, :].astype(LOW)
    total[0] += dot(branch.T, context, NN)

    @pl.when(step == pl.num_programs(0) - 1)
    def _():
        @pl.loop(0, groups * heads)
        def _(j):
            for i in range(3):
                at = pl.multiple_of((2 * place_ref[j] + core) * unit, 8)
                keep_ref[j, i] = total[i, pl.ds(at, unit), :].astype(LOW)
                at = pl.multiple_of((2 * place_ref[j] + 1 - core) * unit, 8)
                send_ref[j, i] = total[i, pl.ds(at, unit), :].astype(LOW)


def middle(core, place, x, g, gain, weight, contexts, unit):
    tokens, width = x.shape
    chips = width // (2 * unit)
    rows = pl.BlockSpec((TILE, width), lambda i, core, place: (i, 0))
    columns = [
        pl.BlockSpec((c.shape[0], TILE), lambda i, core, place: (0, i)) for c in contexts
    ]
    once = pl.Buffered(1)
    half = pl.BlockSpec(
        (chips, 3, unit, width), lambda i, core, place: (0, 0, 0, 0), pipeline_mode=once
    )
    halves = jax.ShapeDtypeStruct((chips, 3, unit, width), LOW)
    return pl.pallas_call(
        functools.partial(middle_kernel, unit, len(contexts)),
        grid_spec=pltpu.PrefetchScalarGridSpec(
            num_scalar_prefetch=2,
            grid=(tokens // TILE,),
            in_specs=[
                rows,
                rows,
                pl.BlockSpec((1, width), lambda i, core, place: (0, 0)),
                pl.BlockSpec(
                    (3, width, width), lambda i, core, place: (0, 0, 0), pipeline_mode=once
                ),
                *columns,
            ],
            out_specs=[
                rows,
                rows,
                *columns,
                half,
                half,
                pl.BlockSpec((8, width), lambda i, core, place: (0, 0)),
            ],
            scratch_shapes=[
                pltpu.VMEM((3, width, width), jnp.float32),
                pltpu.VMEM((width, TILE), jnp.float32),
            ],
        ),
        out_shape=[
            jax.ShapeDtypeStruct((tokens, width), LOW),
            jax.ShapeDtypeStruct((tokens, width), jnp.float32),
            *[jax.ShapeDtypeStruct(c.shape, LOW) for c in contexts],
            halves,
            halves,
            jax.ShapeDtypeStruct((8, width), jnp.float32),
        ],
        compiler_params=pltpu.CompilerParams(vmem_limit_bytes=66_000_000),
        cost_estimate=pl.CostEstimate(
            flops=18 * tokens * width * width,
            bytes_accessed=14 * tokens * width + 12 * width * width,
            transcendentals=tokens * width,
        ),
        name="middle",
    )(core, place, x, g, gain, weight, *contexts)


def back_kernel(groups, x_ref, grad_hidden_ref, gain_ref, *rest):
    w_refs, d_refs, out_ref = rest[: 2 * groups], rest[2 * groups : -1], rest[-1]
    x = x_ref[...].astype(jnp.float32)
    root = lax.rsqrt(mean_rows(x * x) + EPSILON)
    scaled = x * root
    grad_normed = None
    for p in range(groups):
        d = d_refs[p][...].T
        rows = d.shape[1] // 2
        for i in range(2):
            part = dot(d[:, i * rows : (i + 1) * rows], w_refs[2 * p + i][...], NN)
            grad_normed = part if grad_normed is None else grad_normed + part
    w = grad_normed * gain_ref[...]
    out_ref[...] = grad_hidden_ref[...] + root * (w - scaled * mean_rows(w * scaled))


def back(x, grad_hidden, gain, weights, grads):
    tokens, width = x.shape
    rows = pl.BlockSpec((TILE, width), lambda i: (i, 0))
    return pl.pallas_call(
        functools.partial(back_kernel, len(grads)),
        grid=(tokens // TILE,),
        in_specs=[
            rows,
            rows,
            pl.BlockSpec((1, width), lambda i: (0, 0)),
            *[pl.BlockSpec(w.shape, lambda i: (0, 0)) for w in weights],
            *[pl.BlockSpec((d.shape[0], TILE), lambda i: (0, i)) for d in grads],
        ],
        out_specs=rows,
        out_shape=jax.ShapeDtypeStruct((tokens, width), jnp.float32),
        cost_estimate=pl.CostEstimate(
            flops=6 * tokens * width * width, bytes_accessed=18 * tokens * width, transcendentals=0
        ),
        name="back",
    )(x, grad_hidden, gain, *weights, *grads)


def combine_kernel(places, last, keep_ref, came_ref, *refs):
    x_at, z_at, y_at = places
    if x_at is not None:
        came_x, came_y, came_z, *refs = refs
    *out_refs, last_ref = refs[-4:]
    sums = [keep_ref[i, 0].astype(jnp.float32) + came_ref[i, 0].astype(jnp.float32) for i in range(4)]
    if x_at is not None:
        for i in range(2):
            sums[x_at + i] += came_x[i, 0, 0].astype(jnp.float32)
        sums[y_at] += came_y[0, 0].astype(jnp.float32)
        sums[z_at] += came_z[0, 0].astype(jnp.float32)
    if last:
        for ref, value in zip((*out_refs, last_ref), sums):
            ref[0, 0] = value.astype(ref.dtype)
    else:
        out_refs[0][0, 0, 0] = sums[0].astype(LOW)
        out_refs[0][1, 0, 0] = sums[1].astype(LOW)
        out_refs[1][0, 0] = sums[2].astype(LOW)
        out_refs[2][0, 0] = sums[3].astype(LOW)


def combine(kind, group, keep, keep_came, came, into):
    _, three, unit, width = keep.shape
    last = group == 0

    def block(*lead, at=0):
        return pl.BlockSpec((*lead, 1, unit, width), lambda i: (at, *[0] * (len(lead) - 1), i, 0, 0))

    one = pl.BlockSpec((1, 1, unit, width), lambda i: (kind, i, 0, 0))
    two = pl.BlockSpec((2, 1, 1, unit, width), lambda i: (0, kind, i, 0, 0))
    one_shape = jax.ShapeDtypeStruct((2, three, unit, width), LOW)
    two_shape = jax.ShapeDtypeStruct((2, 2, three, unit, width), LOW)
    full_shape = jax.ShapeDtypeStruct((2, three, unit, width), jnp.float32)
    places = (None, None, None) if came is None else (2, FAR[group][1], 3)
    inputs = [keep, keep_came, *(came or [])]
    count = len(inputs)
    shapes = [full_shape, *[one_shape] * 3] if last else [two_shape, one_shape, one_shape]

    def kernel(*refs):
        if into is not None:
            refs = refs[:count] + refs[count + len(into) :]
        if not last:
            refs = (*refs, None)
        combine_kernel(places, last, *refs)

    return pl.pallas_call(
        kernel,
        grid=(three,),
        in_specs=[block(4, at=group if kind else 0)] * 2
        + ([] if came is None else [two, one, one])
        + [pl.BlockSpec(memory_space=pl.ANY)] * len(into or []),
        out_specs=[one] * 4 if last else [two, one, one],
        out_shape=shapes,
        input_output_aliases={count + i: i for i in range(len(into or []))},
        cost_estimate=pl.CostEstimate(
            flops=0, bytes_accessed=20 * three * unit * width, transcendentals=0
        ),
        name="combine",
    )(*inputs, *(into or []))


GROUPS = ((0, 1, 2, 4), (3, 5, 6, 8), (7, 9, 10, 12), (11, 13, 14, 15))
FULL = 32
FAR = ((16, 0), (8, 3), (16, 0))


def exchange(x, bit, n):
    return lax.ppermute(x, AXIS, [(i, i ^ bit) for i in range(n)])


def tie(*values):
    return lax.optimization_barrier(values)


def next_group(group, step, n):
    bit, source = FAR[step]
    return [
        exchange(group[2:4], 2, n),
        exchange(group[3:4], 4, n),
        exchange(group[source : source + 1], bit, n),
    ]


def add(*terms):
    return functools.reduce(jnp.add, [t.astype(jnp.float32) for t in terms])


def sum_four(x, bits, n):
    first, second, third = [exchange(x, bit, n) for bit in bits]
    return (x + first) + (second + third)


def on_device(n, *arguments):
    (
        inputs,
        block_ids,
        cotangent,
        first_gain,
        query_weight,
        key_weight,
        value_weight,
        output_weight,
        second_gain,
        up_weight,
        down_weight,
        query_scale,
    ) = arguments
    seqs, length, width = inputs.shape
    tokens = seqs * length
    depth = query_scale.shape[0]
    unit = depth // 2
    shard = first_gain.shape[0]
    me = lax.axis_index(AXIS)
    whole = n == FULL
    here = me if whole else jnp.zeros_like(me)
    core = (here % 2).reshape(1)
    slots = jnp.array([r for group in GROUPS for r in group], jnp.int32)
    place = jnp.bitwise_xor(here // 2, slots)

    early = jnp.stack([query_weight.T, key_weight.T, value_weight.T])
    late = jnp.stack([output_weight.T, up_weight.T, down_weight.T])
    gains = jnp.concatenate([first_gain, second_gain]).astype(jnp.float32)
    if whole:
        relative = jnp.stack([gains, exchange(gains, 1, n)])
        relative, early = tie(relative, early)
        near = [exchange(relative, b, n) for b in (2, 4, 6)]
        mine = [exchange(early, b, n) for b in (2, 4, 8)]
        near, mine = lax.optimization_barrier((near, mine))
        mine = jnp.stack([early, *mine])
        relative = jnp.concatenate([relative, *near])
        relative = jnp.concatenate([relative] + [exchange(relative, b, n) for b in (8, 16, 24)])
        index = jnp.arange(n)
        chosen = index[:, None] == jnp.bitwise_xor(index, me)[None, :]
        gains = dot(chosen.astype(LOW), relative.astype(LOW), NN)
    else:
        gains = lax.all_gather(gains, AXIS)
    gains = jnp.swapaxes(gains.reshape(n, 2, shard), 0, 1).reshape(2, width)

    ids = block_ids.reshape(1, tokens)
    row = lax.broadcasted_iota(jnp.int32, (EXTRA, tokens), 0)
    qx = ((ids == row) & (row < BLOCKS)).astype(LOW)
    kx = jnp.where(
        row < BLOCKS, jnp.where(ids > row, -1e30, 0.0), jnp.where(row < BLOCKS + 3, 1.0, 0.0)
    ).astype(LOW)
    last = block_ids[:, TILE - 1 :: TILE]
    seen = jnp.sum(block_ids[:, None, :] <= last[:, :, None], axis=-1)
    counts = ((seen + TILE - 1) // TILE).astype(jnp.int32)

    x = inputs.reshape(tokens, width)
    g = cotangent.reshape(tokens, width)
    factor = query_scale / math.sqrt(depth)
    mine_first = jnp.where(core[0] == 0, factor, jnp.roll(factor, unit))
    factor_rows = jnp.broadcast_to(mine_first[:, None], (depth, TILE))

    def forward(mine, other, source, gain=None):
        return attention_forward(
            source, gain, mine.reshape(-1, width), other.reshape(-1, width), factor_rows * LOG2E,
            qx, kx, counts, depth, length,
        )

    mines, others, firsts = [], [], []
    if whole:
        mine, late = tie(mine, late)
        late = lax.all_gather(late, AXIS, axis=1, tiled=True)
        source, gain = x, gains[:1]
        for step in range(4):
            other = exchange(mine, 1, n)
            mines.append(mine)
            others.append(other)
            if step < 3:
                came = next_group(mine, step, n)
            result = forward(mine, other, source, gain)
            if step == 0:
                *result, normed = result
                source, gain = normed, None
            if step < 3:
                *came, first = tie(*came, result[0])
                result = [first, *result[1:]]
                mine = jnp.concatenate(came)
            firsts.append(result)
    else:
        both = lax.all_gather(early, AXIS, axis=1, tiled=True)
        both = both.reshape(3, -1, 2, unit, width)
        source, gain = x, gains[:1]
        for group in GROUPS:
            rows = jnp.stack([both[:, r] for r in group])
            mines.append(rows[:, :, 0])
            others.append(rows[:, :, 1])
            result = forward(mines[-1], others[-1], source, gain)
            if gain is not None:
                *result, normed = result
                source, gain = normed, None
            firsts.append(result)
        late = lax.all_gather(late, AXIS, axis=1, tiled=True)
    contexts = [context for _, context, _ in firsts]
    output, grad_hidden, *rest = middle(core, place, x, g, gains[1:], late, contexts, unit)
    grad_contexts, (keep, send, gain2_rows) = rest[:4], rest[4:]

    def backward(p, grad_context):
        qkv, context, lse = firsts[p]
        mine, other = mines[p].reshape(-1, width), others[p].reshape(-1, width)
        return attention_backward(
            qkv, context, grad_context, lse, qx, kx, counts, factor_rows, normed, mine, other,
            depth, length,
        )

    def small_sums():
        scale_part = jnp.sum(functools.reduce(jnp.add, scale_parts), axis=1)
        scale_part = jnp.where(core[0] == 0, scale_part, jnp.roll(scale_part, unit))
        scale_part = scale_part / (factor * LOG2E) / math.sqrt(depth)
        gain1 = jnp.sum(functools.reduce(jnp.add, gain_parts), axis=0) / gains[0]
        return jnp.concatenate([gain1, jnp.sum(gain2_rows, axis=0), scale_part])

    grads, scale_parts, gain_parts = [None] * 4, [], []
    if whole:
        late_came = exchange(send, 1, n)
        came = away = None
        for p in (3, 2, 1, 0):
            grad_context = grad_contexts[p]
            if away is not None:
                *away, grad_context = tie(*away, grad_context)
            d, part, own_keep, own_send, gain_part = backward(p, grad_context)
            scale_parts.append(part)
            gain_parts.append(gain_part)
            if p == 3:
                late_came, own_send = tie(late_came, own_send)
            else:
                *came, own_send = tie(*came, own_send)
            grads[p] = d
            own_came = exchange(own_send.reshape(4, 3, unit, width), 1, n)
            own_keep = own_keep.reshape(4, 3, unit, width)
            if p == 0:
                small = small_sums()
                small = small + exchange(small, 1, n)
            away = combine(1, p, keep, late_came, came, None)
            if p == 0:
                own_came, small, *away = tie(own_came, small, *away)
                small = sum_four(small, (2, 4, 6), n)
            else:
                own_came, *away = tie(own_came, *away)
            away = combine(0, p, own_keep, own_came, came, away)
            if p == 0:
                final, *away = away
            far = 8 if p == 0 else FAR[p - 1][0]
            came = [exchange(a, bit, n) for a, bit in zip(away, (2, 4, far))]
    else:
        own_rows = []
        for p in range(4):
            grads[p], part, *rows, gain_part = backward(p, grad_contexts[p])
            scale_parts.append(part)
            gain_parts.append(gain_part)
            own_rows.append(jnp.stack(rows).reshape(2, 4, 3, unit, width))
        order = jnp.argsort(slots)
        late_rows = jnp.stack([keep, send], axis=2)[order]
        own_rows = jnp.stack(own_rows).transpose(0, 2, 3, 1, 4, 5)
        own_rows = own_rows.reshape(16, 3, 2, unit, width)[order]
        rows = jnp.concatenate([own_rows, late_rows], axis=1).astype(jnp.float32)
        rows = rows.transpose(1, 0, 2, 3, 4).reshape(6, width, width)
        sums = lax.psum_scatter(rows, AXIS, scatter_dimension=1, tiled=True)
        small = lax.psum(small_sums(), AXIS)

    weights = [w.reshape(-1, width) for pair in zip(mines, others) for w in pair]
    if whole:
        *away, small, grads[0] = tie(*away, small, grads[0])
        small = sum_four(small, (8, 16, 24), n)
    grad_inputs = back(x, grad_hidden, gains[:1], weights, grads)
    if whole:
        *came, small, grad_inputs = tie(*came, small, grad_inputs)
        sums = add(final, *came).reshape(6, unit, width)
    gain1 = lax.dynamic_slice_in_dim(small, me * shard, shard)
    gain2 = lax.dynamic_slice_in_dim(small, width + me * shard, shard)

    return (
        output.reshape(seqs, length, width),
        grad_inputs.reshape(seqs, length, width),
        gain1,
        sums[0].T,
        sums[1].T,
        sums[2].T,
        sums[3].T,
        gain2,
        sums[4].T,
        sums[5].T,
        small[2 * width :],
    )


def solution(mesh):
    rows, columns = P(AXIS), P(None, AXIS)
    in_specs = (rows, rows, rows, rows, *[columns] * 4, rows, columns, columns, P())
    out_specs = (rows, rows, rows, *[columns] * 4, rows, columns, columns, P())
    return jax.shard_map(
        functools.partial(on_device, mesh.shape[AXIS]),
        mesh=mesh,
        in_specs=in_specs,
        out_specs=out_specs,
        check_vma=False,
    )
```
